768 devices in a mesh: seq: 48 (over y_hi, z, core), fsdp: 4 (over x), batch: 4 (over y_lo).
Axes of the slice: x: 4, y: 8 (y_hi: 2, y_lo: 4; y = y_hi * 4 + y_lo), z: 12, core: 2. Of those that a mesh axis runs over, the one named last changes fastest.
Arguments:
- hidden: bfloat16 [16, 6144, 2048], P(('fsdp', 'batch'), 'seq'), may hold values from -6 to 6
- in_weight: bfloat16 [2048, 2208], P(('fsdp', 'batch')), may hold values from -0.125 to 0.125
- read_starts: int32 [16, 4], P(('fsdp', 'batch')), may hold values from 1 to 6143
- conv_weight: float32 [2, 4, 2176], replicated, may hold values from -3 to 3
- conv_bias: float32 [2, 2176], replicated, may hold values from -0.5 to 0.5
- dt_bias: float32 [2, 32], replicated, may hold values from -4.5 to -2.5
- decay: float32 [2, 32], replicated, may hold values from 8.138021e-06 to 0.7
- skip: float32 [2, 32], replicated, may hold values from 0.5 to 1.5
- norm_gain: float32 [2, 2048], replicated, may hold values from 0.5 to 1.5
Outputs:
- mixed: bfloat16 [16, 6144, 2048], P(('fsdp', 'batch'), 'seq')
The draws below stay inside these ranges and needn't reach their ends.
All inputs are finite; a program needn't handle non-finite values.
Results may differ from the reference program's by a relative error of at most 0.0051.
Values may be sent and summed in bfloat16 or wider, within the bound.
A program may use at most 128 MiB of HBM per device.

```python
import math
import jax
import jax.numpy as jnp
from jax import lax

D = 2048
HEADS = 32
HEAD_DIM = 64
STATE = 64
KERNEL = 4
BLOCK = 128
BOUNDS = 4
INNER = 2048
CONV_CH = 2176
PROJ = 2208
LENGTH = 6144
BATCH = 16


def set_ends(entries, stream_key, smallest, high):
    shape = entries.shape
    spot = [jax.random.randint(jax.random.fold_in(stream_key, axis), (), 0, shape[axis]) for axis in range(len(shape))]
    entries = entries.at[tuple(spot)].set(smallest)
    longest = shape.index(max(shape))
    spot[longest] = (spot[longest] + 1) % shape[longest]
    return entries.at[tuple(spot)].set(high)


def shard_levels(rng, extent, shards, low, largest):
    def one(axis_at, blocks):
        draws = jax.random.uniform(jax.random.fold_in(jax.random.fold_in(rng, 6), axis_at), (blocks,), jnp.float32, low / len(shards), largest / len(shards))
        return jnp.repeat(jnp.exp(draws), extent[axis_at] // blocks).reshape((-1,) + (1,) * (len(extent) - axis_at - 1))

    gain = one(*shards[0])
    for cut in shards[1:]:
        gain = gain * one(*cut)
    return gain


def bell_draw(key, dims, deviation, reach, cuts=(), held_as=jnp.bfloat16):
    level = shard_levels(key, dims, cuts, -0.22, 0.18) if cuts else 1.0
    array = jax.random.normal(key, dims, jnp.float32) * deviation * level
    return jnp.minimum(jnp.maximum(array, -reach), reach).astype(held_as)


def setup_inputs(seed: int = 0) -> dict:
    key_list = jax.random.split(jax.random.key(seed), 10)
    return {
        "hidden": bell_draw(key_list[0], (BATCH, LENGTH, D), 1.0, 6.0, ((0, 16), (1, 48))),
        "in_weight": bell_draw(key_list[1], (D, PROJ), D ** -0.5, 0.125, ((0, 16),)),
        "read_starts": set_ends(jax.random.randint(key_list[2], (BATCH, BOUNDS), 1, LENGTH), jax.random.fold_in(key_list[2], 1), 1, LENGTH - 1).astype(jnp.int32),
        "conv_weight": bell_draw(key_list[3], (2, KERNEL, CONV_CH), KERNEL ** -0.5, 3.0, (), jnp.float32),
        "conv_bias": jnp.clip(jax.random.uniform(key_list[4], (2, CONV_CH), jnp.float32, -0.5, 0.5), -0.5, 0.5),
        "dt_bias": jnp.clip(jax.random.uniform(key_list[5], (2, HEADS), jnp.float32, -4.5, -2.5), -4.5, -2.5),
        "decay": jnp.clip(jnp.exp(jax.random.uniform(key_list[6], (2, HEADS), jnp.float32, math.log(8.138021257764194e-06), math.log(0.7))), 8.138021257764194e-06, 0.7),
        "skip": jnp.clip(jax.random.uniform(key_list[7], (2, HEADS), jnp.float32, 0.5, 1.5), 0.5, 1.5),
        "norm_gain": jnp.clip(1.0 + 0.1 * jax.random.normal(key_list[8], (2, INNER), jnp.float32), 0.5, 1.5),
    }


def conv_silu(padded, weight, bias):
    length = padded.shape[0] - weight.shape[0] + 1
    total = jnp.broadcast_to(bias[None, :], (length, bias.shape[0]))
    for tap in range(weight.shape[0]):
        total = total + weight[tap][None, :] * padded[tap:tap + length].astype(jnp.float32)
    return jax.nn.silu(total).astype(jnp.bfloat16)

def block_parts(x_part, b_part, c_part, step_size, log_rate, resets):
    length = x_part.shape[0]
    running = jnp.cumsum(log_rate, axis=0)
    resets_seen = jnp.cumsum(resets)
    scores = jnp.dot(c_part, b_part.T, preferred_element_type=jnp.float32)
    positions = jnp.arange(length)
    allowed = (positions[:, None] >= positions[None, :]) & (resets_seen[:, None] == resets_seen[None, :])
    log_gaps = jnp.minimum(running[:, None, :] - running[None, :, :], 0.0)
    weights = jnp.where(allowed[:, :, None], jnp.exp(log_gaps), 0.0) * scores[:, :, None] * step_size[None, :, :]
    weights = weights.astype(jnp.bfloat16)
    values = x_part.reshape(length, HEADS, HEAD_DIM)
    inner_part = jnp.einsum('tsh,shp->thp', weights.astype(jnp.float32), values.astype(jnp.float32), precision=lax.Precision.HIGHEST)
    last_same = resets_seen == resets_seen[-1]
    tail_weight = jnp.where(last_same[:, None], jnp.exp(running[-1][None, :] - running), 0.0) * step_size
    inputs = (tail_weight[:, :, None] * values.astype(jnp.float32)).astype(jnp.bfloat16)
    local_end = jnp.einsum('shp,sn->hpn', inputs.astype(jnp.float32), b_part.astype(jnp.float32), precision=lax.Precision.HIGHEST)
    lead_fade = jnp.where((resets_seen == 0)[:, None], jnp.exp(running), 0.0)
    block_fade = jnp.where(resets_seen[-1] == 0, jnp.exp(running[-1]), 0.0)
    return (inner_part, local_end, lead_fade, block_fade)

def direction(conv_out, step_cols, resets, bias_step, rates, direct, gains):
    length = conv_out.shape[0]
    blocks = length // BLOCK
    step_size = jax.nn.softplus(step_cols.astype(jnp.float32) + bias_step[None, :])
    log_rate = -step_size * rates[None, :]
    items = (conv_out[:, :INNER].reshape(blocks, BLOCK, INNER), conv_out[:, INNER:INNER + STATE].reshape(blocks, BLOCK, STATE), conv_out[:, INNER + STATE:].reshape(blocks, BLOCK, STATE), step_size.reshape(blocks, BLOCK, HEADS), log_rate.reshape(blocks, BLOCK, HEADS), resets.reshape(blocks, BLOCK))

    def one_block(state, item):
        x_part, b_part, c_part, step_here, rate_here, reset_here = item
        inner_part, local_end, lead_fade, block_fade = block_parts(x_part, b_part, c_part, step_here, rate_here, reset_here)
        rounded = lax.optimization_barrier(state.astype(jnp.bfloat16)).astype(jnp.float32)
        carried = jnp.einsum('tn,hpn->thp', c_part.astype(jnp.float32), rounded, precision=lax.Precision.HIGHEST)
        direct_part = direct[None, :, None] * x_part.reshape(BLOCK, HEADS, HEAD_DIM).astype(jnp.float32)
        output = inner_part + lead_fade[:, :, None] * carried + direct_part
        return (block_fade[:, None, None] * state + local_end, output)
    start_state = jnp.zeros((HEADS, HEAD_DIM, STATE), jnp.float32)
    _, outputs = lax.scan(one_block, start_state, items)
    result = outputs.reshape(length, HEADS, HEAD_DIM)
    scale = lax.rsqrt(lax.optimization_barrier(jnp.mean(result * result, axis=-1, keepdims=True)) + 1e-05)
    return (result * scale * gains.reshape(HEADS, HEAD_DIM)).reshape(length, INNER)

def reference(hidden, in_weight, read_starts, conv_weight, conv_bias, dt_bias, decay, skip, norm_gain):

    def one_sequence(item):
        tokens, marks = item
        projected = jnp.dot(tokens, in_weight, preferred_element_type=jnp.float32).astype(jnp.bfloat16)
        positions = jnp.arange(LENGTH, dtype=jnp.int32)
        starts_here = jnp.any(positions[:, None] == marks[None, :], axis=1).astype(jnp.float32)
        starts_next = jnp.any((positions + 1)[:, None] == marks[None, :], axis=1).astype(jnp.float32)
        xbc = projected[:, :CONV_CH]
        margin = KERNEL - 1
        zero_rows = jnp.zeros((margin, CONV_CH), jnp.bfloat16)
        forward_in = conv_silu(jnp.concatenate([zero_rows, xbc], axis=0), conv_weight[0], conv_bias[0])
        backward_in = conv_silu(jnp.flip(jnp.concatenate([xbc, zero_rows], axis=0), 0), conv_weight[1], conv_bias[1])
        step_cols = projected[:, CONV_CH:]
        forward_out = direction(forward_in, step_cols, starts_here, dt_bias[0], decay[0], skip[0], norm_gain[0])
        backward_out = direction(backward_in, jnp.flip(step_cols, 0), jnp.flip(starts_next, 0), dt_bias[1], decay[1], skip[1], norm_gain[1])
        return (forward_out + jnp.flip(backward_out, 0)).astype(jnp.bfloat16)
    return lax.map(one_sequence, (hidden, read_starts))
```

```python
import functools

import jax
import jax.numpy as jnp
from jax import lax
from jax.experimental import pallas as pl
from jax.experimental.pallas import tpu as pltpu
from jax.sharding import PartitionSpec as P

MESH = pl.DeviceIdType.MESH
HEADS = 32
HEAD_DIM = 64
STATE = 64
BLOCK = 128
INNER = 2048
HALF = 1024
COLS = 1280
HALO = 16
ROWS = 2 * BLOCK + 2 * HALO
F32 = jnp.float32
BF16 = jnp.bfloat16


def kernel(
    cfg,
    hid_ref,
    w_ref,
    marks_ref,
    cw_ref,
    cb_ref,
    dtb_ref,
    dec_ref,
    skip_ref,
    gain_ref,
    out_ref,
    wb,
    hidb,
    proj,
    xs,
    ys,
    lk,
    ls,
    fs,
    fb,
    r1,
    rf1,
    gb,
    gf,
    tb,
    tr,
    o4,
    sin,
    outb,
    par,
    cum_s,
    cumt_s,
    stept_s,
    tail_s,
    lead_s,
    msc_s,
    bt_s,
    cr_s,
    fade_s,
    w_ss,
    w_rs,
    h_ss,
    h_rs,
    l_ss,
    l_rs,
    g_ss,
    g_rs,
    o_sem,
):
    nx, ny, nz, zl, zh_n, seqs = cfg
    ql = HALF // zl
    tq = ql // 128
    s = lax.axis_index("seq")
    x = lax.axis_index("fsdp")
    y = lax.axis_index("batch")
    core = lax.rem(s, 2)
    chip = lax.div(s, 2)
    chips = seqs // 2
    z = lax.rem(chip, nz)
    yh = lax.div(chip, nz)
    q = lax.rem(z, zl)
    zh = lax.div(z, zl)

    def dev(seq, xx=x, yy=y):
        return {"seq": seq, "fsdp": xx, "batch": yy}

    def at_z(zz):
        return dev((yh * nz + zz) * 2 + core)

    partner = dev(chip * 2 + 1 - core)
    xp, xm = dev(s, lax.rem(x + 1, nx)), dev(s, lax.rem(x + nx - 1, nx))
    wrap_p = lax.div(y + 1, ny)
    wrap_m = 1 - lax.div(y + ny - 1, ny)
    yp = dev(lax.rem(s + (seqs // 2) * wrap_p, seqs), x, lax.rem(y + 1, ny))
    ym = dev(lax.rem(s + (seqs // 2) * wrap_m, seqs), x, lax.rem(y + ny - 1, ny))
    nxt = lax.rem(chip + 1, chips)
    prv = lax.rem(chip + chips - 1, chips)
    zl_peers = [at_z(zh * zl + lax.rem(q + k, zl)) for k in range(1, zl)]
    zh_peers = [at_z(lax.rem(zh + k, zh_n) * zl + q) for k in range(1, zh_n)]
    y_peer = dev(((1 - yh) * nz + z) * 2 + core)

    kb = w_ref.shape[0]
    wb[0, 0, :, 0:HALF] = w_ref[:, pl.ds(pl.multiple_of(core * HALF, HALF), HALF)]
    wb[0, 0, :, HALF : HALF + 128] = w_ref[:, INNER : INNER + 128]
    wb[0, 0, :, HALF + 128 :] = jnp.zeros((kb, 128), BF16)
    wb[0, 0, :, HALF + 128 : HALF + 160] = w_ref[:, INNER + 128 : INNER + 160]
    par[...] = jnp.zeros_like(par)
    par[0:2, 0:HEADS] = dtb_ref[...]
    par[2:4, 0:HEADS] = dec_ref[...]
    fs[...] = jnp.zeros_like(fs)
    own_rows = pl.ds(pl.multiple_of(HALO + core * BLOCK, HALO), BLOCK)
    hidb[own_rows, :] = hid_ref[0]

    barrier = pltpu.get_barrier_semaphore()
    greet = [partner, dev(nxt * 2), dev(nxt * 2 + 1), dev(prv * 2), dev(prv * 2 + 1)]
    greet += zl_peers + zh_peers + [y_peer]
    if nx > 1:
        greet += [xp, xm, yp, ym]
    for peer in greet:
        pl.semaphore_signal(barrier, inc=1, device_id=peer, device_id_type=MESH)
    pl.semaphore_wait(barrier, len(greet))

    def remote(src, dst, ssem, rsem, peer):
        return pltpu.make_async_remote_copy(
            src_ref=src,
            dst_ref=dst,
            send_sem=ssem,
            recv_sem=rsem,
            device_id=peer,
            device_id_type=MESH,
        )

    sent = []

    msgs = {}

    def w_send(half, a, b, r0, n, axis, step, tag):
        swap = half == 1
        dim_x = (axis == 1) != swap
        i, j = (b, a) if swap else (a, b)
        ii = (i + step) % nx if dim_x else i
        jj = j if dim_x else (j + step) % ny
        peer = (xp if step > 0 else xm) if dim_x else (yp if step > 0 else ym)
        k = len(msgs)
        rows = pl.ds(half * (kb // 2) + r0, n)
        copy = remote(wb.at[i, j, rows, :], wb.at[ii, jj, rows, :], w_ss.at[k], w_rs.at[k], peer)
        copy.start()
        sent.append(copy)
        aa, bb = (jj, ii) if swap else (ii, jj)
        msgs[(half, aa, bb, tag)] = copy

    def w_wait(half, a, b, tag=0):
        msgs[(half, a, b, tag)].wait_recv()

    hk = kb // 2
    halves = (0, 1)
    if nx > 1:
        for h in halves:
            w_send(h, 0, 0, 0, hk, 1, 1, 0)
            w_send(h, 0, 0, 0, hk, 1, -1, 0)

    pc = remote(hid_ref.at[0], hidb.at[own_rows, :], h_ss.at[0], h_rs.at[0], partner)
    pc.start()
    sent.append(pc)
    target = core * nxt + (1 - core) * prv
    src_rows = pl.ds(pl.multiple_of((BLOCK - HALO) * core, HALO), HALO)
    dst_rows = pl.ds(pl.multiple_of((HALO + 2 * BLOCK) * (1 - core), HALO), HALO)
    for c in range(2):
        copy = remote(
            hid_ref.at[0, src_rows, :],
            hidb.at[dst_rows, :],
            h_ss.at[1 + c],
            h_rs.at[2 - core],
            dev(target * 2 + c),
        )
        copy.start()
        sent.append(copy)

    if nx > 1:
        for h in halves:
            w_send(h, 0, 0, 0, hk, 2, 1, 0)
            w_send(h, 0, 0, 0, hk, 2, -1, 0)
        for h in halves:
            w_wait(h, 1, 0)
            w_send(h, 1, 0, 0, hk // 2, 1, 1, 0)
            w_wait(h, 3, 0)
            w_send(h, 3, 0, hk // 2, hk // 2, 1, -1, 1)
        for h in halves:
            for a in (1, 3):
                w_send(h, a, 0, 0, hk, 2, 1, 0)
                w_send(h, a, 0, 0, hk, 2, -1, 0)
        for h in halves:
            w_wait(h, 0, 1)
            w_send(h, 0, 1, 0, hk, 2, 1, 0)
        for h in halves:
            w_wait(h, 2, 0, 0)
            w_wait(h, 2, 0, 1)
            w_send(h, 2, 0, 0, hk, 2, 1, 0)
            w_send(h, 2, 0, 0, hk, 2, -1, 0)
        for h in halves:
            w_wait(h, 1, 1)
            w_send(h, 1, 1, 0, hk, 2, 1, 0)
            w_wait(h, 3, 3)
            w_send(h, 3, 3, 0, hk, 2, -1, 0)
        for h in halves:
            w_wait(h, 2, 3)
            w_send(h, 2, 3, 0, hk, 2, -1, 0)
        for h in halves:
            for a, b in ((0, 3), (1, 3), (3, 1), (2, 1), (0, 2), (1, 2), (3, 2), (2, 2)):
                w_wait(h, a, b)

    pc.wait_recv()
    for side in range(2):
        rows = pl.ds((HALO + 2 * BLOCK) * side, HALO)
        remote(
            hid_ref.at[0, 0:HALO, :], hidb.at[rows, :], h_ss.at[1], h_rs.at[1 + side], partner
        ).wait_recv()

    proj[...] = jnp.zeros_like(proj)
    if nx > 1:

        @pl.loop(0, nx * ny // 2)
        def _(t):
            i = lax.div(t, ny // 2)
            j = lax.rem(t, ny // 2) * 2
            kx = lax.rem(x + nx - i, nx) * ny
            k0 = kx + lax.rem(y + ny - j, ny)
            k1 = kx + lax.rem(y + ny - j - 1, ny)
            left = jnp.concatenate(
                [
                    hidb[:, pl.ds(pl.multiple_of(k0 * kb, kb), kb)],
                    hidb[:, pl.ds(pl.multiple_of(k1 * kb, kb), kb)],
                ],
                axis=1,
            )
            right = wb[i, pl.ds(j, 2)].reshape(2 * kb, COLS)
            proj[...] += jnp.dot(left, right, preferred_element_type=F32)

    else:
        proj[...] = jnp.dot(hidb[...], wb[0, 0], preferred_element_type=F32)
    proj[...] = proj[...].astype(BF16).astype(F32)
    first_f = jnp.where(chip == 0, 0.0, 1.0)
    last_f = jnp.where(chip == chips - 1, 0.0, 1.0)
    proj[0:HALO, :] = proj[0:HALO, :] * first_f
    proj[HALO + 2 * BLOCK :, :] = proj[HALO + 2 * BLOCK :, :] * last_f

    def conv(d, lanes, wlanes):
        total = jnp.broadcast_to(cb_ref[d : d + 1, wlanes], (2 * BLOCK, 128))
        for k in range(4):
            r0 = HALO - 3 + k if d == 0 else HALO + 3 - k
            total = total + cw_ref[d, k : k + 1, wlanes] * proj[pl.ds(r0, 2 * BLOCK), lanes]
        return total * jax.nn.sigmoid(total)

    row_i = lax.broadcasted_iota(jnp.int32, (128, 128), 0)
    lane_i = lax.broadcasted_iota(jnp.int32, (128, 128), 1)
    low = lane_i < HEAD_DIM
    low1 = lax.broadcasted_iota(jnp.int32, (1, 128), 1) < HEAD_DIM

    def seg_at(v):
        total = jnp.int32(0)
        for m in range(4):
            total = total + jnp.where(marks_ref[0, m] <= v, 1, 0)
        return total

    for d in range(2):
        bc = conv(d, slice(HALF, HALF + 128), slice(INNER, INNER + 128))
        pd = par[d : d + 1, :]
        pr = par[2 + d : 3 + d, :]
        pd = jnp.where(core == 0, pd, pltpu.roll(pd, 112, 1))
        pr = jnp.where(core == 0, pr, pltpu.roll(pr, 112, 1))
        tri = (lane_i <= row_i) if d == 0 else (lane_i >= row_i)
        trif = jnp.where(tri, 1.0, 0.0)
        for j in range(2):
            n = d * 2 + j
            t0 = chip * (2 * BLOCK) + j * BLOCK
            st = proj[HALO + j * BLOCK : HALO + (j + 1) * BLOCK, HALF + 128 :]
            st = jnp.where(core == 0, st, pltpu.roll(st, 112, 1))
            pre = st + pd
            step = jnp.maximum(pre, 0.0) + jnp.log1p(jnp.exp(-jnp.abs(pre)))
            rate = -step * pr
            cum = jnp.dot(
                trif, rate, preferred_element_type=F32, precision=lax.Precision.HIGHEST
            )
            cum_s[n] = cum
            cumt_s[n] = cum.T
            stept_s[n] = step.T
            seg_r = jnp.zeros((128, 128), jnp.int32)
            seg_c = jnp.zeros((128, 128), jnp.int32)
            for m in range(4):
                mark = marks_ref[0, m] - t0
                seg_r = seg_r + jnp.where(row_i >= mark, 1, 0)
                seg_c = seg_c + jnp.where(lane_i >= mark, 1, 0)
            in_seg, out_seg = (
                (seg_at(t0 - 1), seg_at(t0 + BLOCK - 1))
                if d == 0
                else (seg_at(t0 + BLOCK), seg_at(t0))
            )
            base = seg_at(t0 - 1) * 0
            last = cum[BLOCK - 1 : BLOCK, :] if d == 0 else cum[0:1, :]
            lead_s[n] = jnp.where(seg_r == in_seg - base, jnp.exp(cum), 0.0)
            tail_s[n] = jnp.where(seg_r == out_seg, jnp.exp(last - cum), 0.0) * step
            same = jnp.where(in_seg == out_seg, 1.0, 0.0)
            fade_s[n : n + 1, :] = jnp.exp(last) * same
            bcj = bc[j * BLOCK : (j + 1) * BLOCK, :]
            b_only = jnp.where(low, bcj, 0.0).astype(BF16)
            c_low = pltpu.roll(bcj, HEAD_DIM, 1).astype(BF16)
            scores = lax.dot_general(
                c_low, b_only, (((1,), (1,)), ((), ())), preferred_element_type=F32
            )
            msc_s[n] = jnp.where(tri & (seg_r == seg_c), scores, 0.0)
            bt_s[n] = bcj.T[0:STATE, :].astype(BF16)
            cr_s[n] = c_low

    def pair(value, mask):
        return jnp.where(mask, value[:, 0:1], value[:, 1:2])

    def lanes_of(p):
        return pl.ds(pl.multiple_of(p * 128, 128), 128)

    order = ((0, 1), (1, 0))

    @pl.loop(0, HALF // 128)
    def _(p):
        lanes = lanes_of(p)
        wl = pl.ds(pl.multiple_of(core * HALF + p * 128, 128), 128)
        quarter = lax.div(p, tq)
        inner = pl.ds(pl.multiple_of(lax.rem(p, tq) * 128, 128), 128)
        shift = 128 - 2 * p
        fades = pltpu.roll(fade_s[...], shift, 1)
        for d in range(2):
            xc = conv(d, lanes, wl).astype(BF16)
            xs[d, :, lanes] = xc
            ends = []
            for j in range(2):
                tails = pair(pltpu.roll(tail_s[d * 2 + j], shift, 1), low)
                inp = (tails * xc[j * BLOCK : (j + 1) * BLOCK, :].astype(F32)).astype(BF16)
                ends.append(jnp.dot(bt_s[d * 2 + j], inp, preferred_element_type=F32))
            f, g = order[d]
            fade_f = pair(fades[d * 2 + f : d * 2 + f + 1, :], low1)
            fade_g = pair(fades[d * 2 + g : d * 2 + g + 1, :], low1)
            lk[d, :, lanes] = ends[f]
            fb[d : d + 1, lanes] = fade_f
            ls[quarter, d, :, inner] = (fade_g * ends[f] + ends[g]).astype(BF16)
            fs[quarter, d : d + 1, inner] = fade_f * fade_g

    def local_pairs(lo, hi):
        @pl.loop(lo, hi)
        def _(p):
            lanes = lanes_of(p)
            shift = 128 - 2 * p
            head = core * (HEADS // 2) + 2 * p
            for d in range(2):
                skips = jnp.where(low1, skip_ref[d, head], skip_ref[d, head + 1])
                for j in range(2):
                    n = d * 2 + j
                    rows = slice(j * BLOCK, (j + 1) * BLOCK)
                    xt = xs[d, rows, lanes]
                    cums = pltpu.roll(cum_s[n], shift, 1)
                    ws = []
                    for hh in range(2):
                        h = pl.ds(2 * p + hh, 1)
                        gap = jnp.minimum(cums[:, hh : hh + 1] - cumt_s[n, h, :], 0.0)
                        ws.append((jnp.exp(gap) * msc_s[n] * stept_s[n, h, :]).astype(BF16))
                    xf = xt.astype(F32)
                    xl = jnp.where(low, xf, 0.0).astype(BF16)
                    xh = jnp.where(low, 0.0, xf).astype(BF16)
                    inner = jnp.dot(
                        jnp.concatenate(ws, axis=1),
                        jnp.concatenate([xl, xh], axis=0),
                        preferred_element_type=F32,
                    )
                    ys[d, rows, lanes] = inner + skips * xf

    copies1 = []
    for k in range(1, zl):
        to = lax.rem(q + k, zl)
        for a, (src, dst) in enumerate(((ls, r1), (fs, rf1))):
            c = remote(
                src.at[to], dst.at[q], l_ss.at[k, a], l_rs.at[k, a], zl_peers[k - 1]
            )
            c.start()
            sent.append(c)
            copies1.append(c)
    r1[q] = ls[q]
    rf1[q] = fs[q]
    local_pairs(0, 4)
    for c in copies1:
        c.wait_recv()

    groups = []
    for d in range(2):
        total = jnp.zeros((STATE, ql), F32)
        fade = jnp.ones((1, ql), F32)
        for step in range(zl):
            c = step if d == 0 else zl - 1 - step
            f = rf1[c, d : d + 1, :]
            total = f * total + r1[c, d].astype(F32)
            fade = fade * f
        gb[zh, d] = total.astype(BF16)
        groups.append(fade)
    gf[zh] = jnp.concatenate(groups + [jnp.zeros((6, ql), F32)], axis=0)
    copies2 = []
    for k in range(1, zh_n):
        for a, buf in enumerate((gb, gf)):
            c = remote(
                buf.at[zh], buf.at[zh], g_ss.at[k, a], g_rs.at[k, a], zh_peers[k - 1]
            )
            c.start()
            sent.append(c)
            copies2.append(c)
    local_pairs(4, 6)
    for c in copies2:
        c.wait_recv()

    for d in range(2):
        total = jnp.zeros((STATE, ql), F32)
        for step in range(zh_n):
            c = step if d == 0 else zh_n - 1 - step
            total = gf[c, d : d + 1, :] * total + gb[c, d].astype(F32)
        tb[d] = total.astype(BF16)
    c3 = remote(tb.at[yh], tr, g_ss.at[0, 0], g_rs.at[0, 0], y_peer)
    c3.start()
    sent.append(c3)
    local_pairs(6, 8)
    c3.wait_recv()

    for d in range(2):
        other = jnp.where(yh == (1 if d == 0 else 0), 1.0, 0.0)
        state = tr[...].astype(F32) * other
        for step in range(zh_n - 1):
            c = step if d == 0 else zh_n - 1 - step
            before = (zh > c) if d == 0 else (zh < c)
            longer = gf[c, d : d + 1, :] * state + gb[c, d].astype(F32)
            state = jnp.where(before, longer, state)
        for step in range(zl):
            c = step if d == 0 else zl - 1 - step
            o4[c, d] = state.astype(BF16)
            if step < zl - 1:
                state = rf1[c, d : d + 1, :] * state + r1[c, d].astype(F32)

    copies4 = []
    for k in range(1, zl):
        to = lax.rem(q + k, zl)
        c = remote(o4.at[to], sin.at[q], l_ss.at[0, k], l_rs.at[0, k], zl_peers[k - 1])
        c.start()
        sent.append(c)
        copies4.append(c)
    sin[q] = o4[q]

    ones = jnp.where((row_i < HEAD_DIM) == low, 1.0 / HEAD_DIM, 0.0).astype(BF16)

    def finish(quarter):
        @pl.loop(0, tq)
        def _(t):
            p = quarter * tq + t
            lanes = lanes_of(p)
            inner = lanes_of(t)
            shift = 128 - 2 * p
            wl = pl.ds(pl.multiple_of(core * HALF + p * 128, 128), 128)
            mixed = [None, None]
            for d in range(2):
                gains = gain_ref[d : d + 1, wl]
                entering = sin[quarter, d, :, inner]
                second = fb[d : d + 1, lanes] * entering.astype(F32) + lk[d, :, lanes]
                f, g = order[d]
                states = {f: entering, g: second.astype(BF16)}
                for j in range(2):
                    n = d * 2 + j
                    rows = slice(j * BLOCK, (j + 1) * BLOCK)
                    carried = jnp.dot(
                        cr_s[n, :, 0:STATE], states[j], preferred_element_type=F32
                    )
                    leads = pair(pltpu.roll(lead_s[n], shift, 1), low)
                    yv = ys[d, rows, lanes] + leads * carried
                    sq = yv * yv
                    hi = sq.astype(BF16)
                    lo = (sq - hi.astype(F32)).astype(BF16)
                    mean = jnp.dot(hi, ones, preferred_element_type=F32) + jnp.dot(
                        lo, ones, preferred_element_type=F32
                    )
                    res = yv * lax.rsqrt(mean + 1e-05) * gains
                    mixed[j] = res if d == 0 else mixed[j] + res
            for j in range(2):
                outb[j, :, lanes] = mixed[j].astype(BF16)

    finish(q)
    for k in range(1, zl):
        copies4[k - 1].wait_recv()
        finish(lax.rem(q + zl - k, zl))

    cols = pl.ds(pl.multiple_of(core * HALF, HALF), HALF)
    oc = remote(outb.at[1 - core], out_ref.at[0, :, cols], o_sem.at[0], o_sem.at[1], partner)
    oc.start()
    own = pltpu.make_async_copy(outb.at[core], out_ref.at[0, :, cols], o_sem.at[2])
    own.start()
    own.wait()
    oc.wait()
    for c in sent:
        c.wait_send()


def solution(mesh):
    nx, ny, seqs = mesh.shape["fsdp"], mesh.shape["batch"], mesh.shape["seq"]
    nz = seqs // 4
    zl = 4 if nz % 4 == 0 and nz > 4 else 2
    zh_n = nz // zl
    ql = HALF // zl
    cfg = (nx, ny, nz, zl, zh_n, seqs)

    def on_device(hidden, in_weight, marks, cw, cb, dtb, dec, skip, gain):
        kb = in_weight.shape[0]
        vmem = pl.BlockSpec(memory_space=pltpu.VMEM)
        smem = pl.BlockSpec(memory_space=pltpu.SMEM)
        dma = pltpu.SemaphoreType.DMA
        return pl.pallas_call(
            functools.partial(kernel, cfg),
            out_shape=jax.ShapeDtypeStruct(hidden.shape, BF16),
            in_specs=[vmem, vmem, smem, vmem, vmem, vmem, vmem, smem, vmem],
            out_specs=pl.BlockSpec(memory_space=pl.ANY),
            scratch_shapes=[
                pltpu.VMEM((nx, ny, kb, COLS), BF16),
                pltpu.VMEM((ROWS, INNER), BF16),
                pltpu.VMEM((ROWS, COLS), F32),
                pltpu.VMEM((2, 2 * BLOCK, HALF), BF16),
                pltpu.VMEM((2, 2 * BLOCK, HALF), F32),
                pltpu.VMEM((2, STATE, HALF), F32),
                pltpu.VMEM((zl, 2, STATE, ql), BF16),
                pltpu.VMEM((zl, 8, ql), F32),
                pltpu.VMEM((8, HALF), F32),
                pltpu.VMEM((zl, 2, STATE, ql), BF16),
                pltpu.VMEM((zl, 8, ql), F32),
                pltpu.VMEM((zh_n, 2, STATE, ql), BF16),
                pltpu.VMEM((zh_n, 8, ql), F32),
                pltpu.VMEM((2, STATE, ql), BF16),
                pltpu.VMEM((STATE, ql), BF16),
                pltpu.VMEM((zl, 2, STATE, ql), BF16),
                pltpu.VMEM((zl, 2, STATE, ql), BF16),
                pltpu.VMEM((2, BLOCK, HALF), BF16),
                pltpu.VMEM((8, 128), F32),
                pltpu.VMEM((4, 128, 128), F32),
                pltpu.VMEM((4, 128, 128), F32),
                pltpu.VMEM((4, 128, 128), F32),
                pltpu.VMEM((4, 128, 128), F32),
                pltpu.VMEM((4, 128, 128), F32),
                pltpu.VMEM((4, 128, 128), F32),
                pltpu.VMEM((4, STATE, 128), BF16),
                pltpu.VMEM((4, 128, 128), BF16),
                pltpu.VMEM((8, 128), F32),
                dma((40,)),
                dma((40,)),
                dma((3,)),
                dma((3,)),
                dma((4, 4)),
                dma((4, 4)),
                dma((3, 2)),
                dma((3, 2)),
                dma((3,)),
            ],
            compiler_params=pltpu.CompilerParams(
                collective_id=0, has_side_effects=True, vmem_limit_bytes=48 * 1024 * 1024
            ),
        )(hidden, in_weight, marks, cw, cb, dtb, dec, skip, gain)

    group = P(("fsdp", "batch"), "seq", None)
    rows = P(("fsdp", "batch"), None)
    return jax.shard_map(
        on_device,
        mesh=mesh,
        in_specs=(group, rows, rows, P(), P(), P(), P(), P(), P()),
        out_specs=group,
        check_vma=False,
    )
```

```python
import functools

import jax
import jax.numpy as jnp
from jax import lax
from jax.experimental import pallas as pl
from jax.experimental.pallas import tpu as pltpu
from jax.sharding import PartitionSpec as P

MESH = pl.DeviceIdType.MESH
HEADS = 32
HEAD_DIM = 64
STATE = 64
BLOCK = 128
INNER = 2048
HALF = 1024
PART = 384
HALO = 16
ROWS = 2 * BLOCK + 2 * HALO
F32 = jnp.float32
BF16 = jnp.bfloat16


def kernel(
    cfg,
    hid_ref,
    w_ref,
    marks_ref,
    cw_ref,
    cb_ref,
    dtb_ref,
    dec_ref,
    skip_ref,
    gain_ref,
    out_ref,
    wb,
    hidb,
    proj,
    tile,
    other,
    xs,
    ys,
    lk,
    ls,
    fs,
    fb,
    r1,
    rf1,
    gb,
    gf,
    tb,
    tr,
    o4,
    sin,
    outb,
    par,
    cum_s,
    cumt_s,
    stept_s,
    tail_s,
    lead_s,
    msc_s,
    bt_s,
    cr_s,
    fade_s,
    w_ss,
    w_rs,
    h_ss,
    h_rs,
    l_ss,
    l_rs,
    g_ss,
    g_rs,
    in_sem,
    o_ss,
    o_rs,
    own_sem,
):
    nx, ny, nz, zl, zh_n, seqs = cfg
    ql = HALF // zl
    tq = ql // 128
    s = lax.axis_index("seq")
    x = lax.axis_index("fsdp")
    y = lax.axis_index("batch")
    core = lax.rem(s, 2)
    chip = lax.div(s, 2)
    chips = seqs // 2
    z = lax.rem(chip, nz)
    yh = lax.div(chip, nz)
    q = lax.rem(z, zl)
    zh = lax.div(z, zl)

    def dev(seq, xx=x, yy=y):
        return {"seq": seq, "fsdp": xx, "batch": yy}

    def at_z(zz):
        return dev((yh * nz + zz) * 2 + core)

    partner = dev(chip * 2 + 1 - core)
    xp, xm = dev(s, lax.rem(x + 1, nx)), dev(s, lax.rem(x + nx - 1, nx))
    wrap_p = lax.div(y + 1, ny)
    wrap_m = 1 - lax.div(y + ny - 1, ny)
    yp = dev(lax.rem(s + (seqs // 2) * wrap_p, seqs), x, lax.rem(y + 1, ny))
    ym = dev(lax.rem(s + (seqs // 2) * wrap_m, seqs), x, lax.rem(y + ny - 1, ny))
    nxt = lax.rem(chip + 1, chips)
    prv = lax.rem(chip + chips - 1, chips)
    rot = lax.rem(z, 3) if nx > 1 else jnp.int32(0)
    zp, zm = at_z(lax.rem(z + 1, nz)), at_z(lax.rem(z + nz - 1, nz))
    zl_peers = [at_z(zh * zl + lax.rem(q + k, zl)) for k in range(1, zl)]
    zh_peers = [at_z(lax.rem(zh + k, zh_n) * zl + q) for k in range(1, zh_n)]
    y_peer = dev(((1 - yh) * nz + z) * 2 + core)

    barrier = pltpu.get_barrier_semaphore()
    greet = [partner, dev(nxt * 2), dev(nxt * 2 + 1), dev(prv * 2), dev(prv * 2 + 1)]
    greet += zl_peers + zh_peers + [y_peer]
    if nx > 1:
        greet += [xp, xm, yp, ym, zp, zm]
    for peer in greet:
        pl.semaphore_signal(barrier, inc=1, device_id=peer, device_id_type=MESH)

    own_rows = pl.ds(pl.multiple_of(HALO + core * BLOCK, HALO), BLOCK)
    kb = w_ref.shape[1]
    reads = [(hid_ref.at[0], hidb.at[own_rows, :])]
    part_lanes = [
        pl.ds(pl.multiple_of(lax.rem(rot + u, 3) * PART, PART), PART) for u in (1, 2, 0)
    ]
    bases = [lax.rem(p + 5 - rot, 3) * PART for p in range(3)]
    cols0 = core * HALF
    for src, dst, count in (
        (cols0, bases[0], PART),
        (cols0 + PART, bases[1], PART),
        (cols0 + 2 * PART, bases[2], 256),
        (INNER + 128 * core, bases[2] + 256, 32),
        (INNER + 32, bases[2] + 288, 96),
    ):
        reads.append(
            (
                w_ref.at[pl.ds(pl.multiple_of(src, 32), count), :],
                wb.at[0, 0, pl.ds(pl.multiple_of(dst, 32), count), :],
            )
        )
    reads = [pltpu.make_async_copy(a, b, in_sem.at[k]) for k, (a, b) in enumerate(reads)]
    for c in reads:
        c.start()
    par[...] = jnp.zeros_like(par)
    par[0:2, 0:HEADS] = dtb_ref[...]
    par[2:4, 0:HEADS] = dec_ref[...]
    fade_s[...] = jnp.zeros_like(fade_s)
    for c in reads:
        c.wait()
    pl.semaphore_wait(barrier, len(greet))

    def remote(src, dst, ssem, rsem, peer):
        return pltpu.make_async_remote_copy(
            src_ref=src,
            dst_ref=dst,
            send_sem=ssem,
            recv_sem=rsem,
            device_id=peer,
            device_id_type=MESH,
        )

    sent = []

    msgs = {}
    zmsgs = {}

    def w_send(half, a, b, r0, n, axis, step, tag):
        swap = half == 1
        dim_x = (axis == 1) != swap
        i, j = (b, a) if swap else (a, b)
        ii = (i + step) % nx if dim_x else i
        jj = j if dim_x else (j + step) % ny
        peer = (xp if step > 0 else xm) if dim_x else (yp if step > 0 else ym)
        k = len(msgs)
        rows = pl.ds(half * PART + r0, n)
        copy = remote(
            wb.at[i, j, rows, :], wb.at[ii, jj, rows, :], w_ss.at[k], w_rs.at[k], peer
        )
        copy.start()
        sent.append(copy)
        aa, bb = (jj, ii) if swap else (ii, jj)
        msgs[(half, aa, bb, tag)] = copy

    def w_wait(half, a, b):
        for tag in range(2):
            if (half, a, b, tag) in msgs:
                msgs[(half, a, b, tag)].wait_recv()
        i, j = (b, a) if half == 1 else (a, b)
        k = 32 + len(zmsgs)
        copy = remote(
            wb.at[i, j, pl.ds(half * (PART + hk // 2), hk // 2), :],
            wb.at[i, j, pl.ds(2 * PART + half * (hk // 2), hk // 2), :],
            w_ss.at[k],
            w_rs.at[k],
            zm if half else zp,
        )
        copy.start()
        sent.append(copy)
        zmsgs[(half, i, j)] = copy

    hk = PART
    halves = (0, 1)
    if nx > 1:
        for h in halves:
            w_send(h, 0, 0, 0, hk, 1, 1, 0)
            w_send(h, 0, 0, 0, hk, 1, -1, 0)

    pc = remote(hid_ref.at[0], hidb.at[own_rows, :], h_ss.at[0], h_rs.at[0], partner)
    pc.start()
    sent.append(pc)
    target = core * nxt + (1 - core) * prv
    src_rows = pl.ds(pl.multiple_of((BLOCK - HALO) * core, HALO), HALO)
    dst_rows = pl.ds(pl.multiple_of((HALO + 2 * BLOCK) * (1 - core), HALO), HALO)
    for c in range(2):
        copy = remote(
            hid_ref.at[0, src_rows, :],
            hidb.at[dst_rows, :],
            h_ss.at[1 + c],
            h_rs.at[2 - core],
            dev(target * 2 + c),
        )
        copy.start()
        sent.append(copy)

    def rows_wait():
        pc.wait_recv()
        for side in range(2):
            rows = pl.ds((HALO + 2 * BLOCK) * side, HALO)
            remote(
                hid_ref.at[0, 0:HALO, :], hidb.at[rows, :], h_ss.at[1], h_rs.at[1 + side], partner
            ).wait_recv()

    def project(slots, parts, first=False):
        left = []
        for i, j in slots:
            k = lax.rem(x + nx - i, nx) * ny + lax.rem(y + ny - j, ny)
            left.append(hidb[:, pl.ds(pl.multiple_of(k * kb, kb), kb)])
        left = jnp.concatenate(left, axis=1)
        for u in parts:
            rows = slice(u * PART, (u + 1) * PART)
            right = jnp.concatenate([wb[i, j, rows, :] for i, j in slots], axis=1)
            value = lax.dot_general(
                left, right, (((1,), (1,)), ((), ())), preferred_element_type=F32
            )
            if first:
                proj[:, part_lanes[u]] = value
            else:
                proj[:, part_lanes[u]] += value

    if nx > 1:
        xy, zz = (0, 1), (2,)
        order_k = (
            ((0, 0), (0, 1)),
            ((1, 0), (0, 3)),
            ((3, 0), (1, 1)),
            ((3, 3), (1, 3)),
            ((3, 1), (0, 2)),
            ((2, 0), (2, 1)),
            ((1, 2), (3, 2)),
            ((2, 3), (2, 2)),
        )
        for h in halves:
            w_send(h, 0, 0, 0, hk, 2, 1, 0)
            w_send(h, 0, 0, 0, hk, 2, -1, 0)
        for h in halves:
            w_wait(h, 1, 0)
            w_send(h, 1, 0, 0, hk // 2, 1, 1, 0)
            w_wait(h, 3, 0)
            w_send(h, 3, 0, hk // 2, hk // 2, 1, -1, 1)
        for h in halves:
            for a in (1, 3):
                w_send(h, a, 0, 0, hk, 2, 1, 0)
                w_send(h, a, 0, 0, hk, 2, -1, 0)
        rows_wait()
        for h in halves:
            w_wait(h, 0, 1)
            w_send(h, 0, 1, 0, hk, 2, 1, 0)
            w_wait(h, 0, 3)
        project(order_k[0], xy, True)
        for h in halves:
            w_wait(h, 2, 0)
            w_send(h, 2, 0, 0, hk, 2, 1, 0)
            w_send(h, 2, 0, 0, hk, 2, -1, 0)
        project(order_k[1], xy)
        for h in halves:
            w_wait(h, 1, 1)
            w_send(h, 1, 1, 0, hk, 2, 1, 0)
            w_wait(h, 3, 3)
            w_send(h, 3, 3, 0, hk, 2, -1, 0)
        project(order_k[2], xy)
        for h in halves:
            w_wait(h, 1, 3)
            w_wait(h, 3, 1)
        project(order_k[3], xy)
        for h in halves:
            w_wait(h, 2, 3)
            w_send(h, 2, 3, 0, hk, 2, -1, 0)
            w_wait(h, 0, 2)
        project(order_k[4], xy)
        for h in halves:
            w_wait(h, 2, 1)
            w_wait(h, 1, 2)
        project(order_k[5], xy)

        def z_wait(slots):
            for i, j in slots:
                for h in halves:
                    if (i, j) != (0, 0):
                        zmsgs[(h, i, j)].wait_recv()

        z_wait(order_k[0])
        project(order_k[0], zz, True)
        z_wait(order_k[1])
        project(order_k[1], zz)
        for h in halves:
            w_wait(h, 3, 2)
        project(order_k[6], xy)
        for h in halves:
            w_wait(h, 2, 2)
        project(order_k[7], xy)
        for slots in order_k[2:]:
            z_wait(slots)
            project(slots, zz)
    else:
        rows_wait()
        project(((0, 0),), (0, 1, 2), True)

    tile[...] = proj[:, HALF : HALF + 128].astype(BF16)
    swap_tile = remote(tile, other, h_ss.at[3], h_rs.at[3], partner)
    swap_tile.start()
    sent.append(swap_tile)
    first_f = jnp.where(chip == 0, 0.0, 1.0)
    last_f = jnp.where(chip == chips - 1, 0.0, 1.0)

    def ends_off(lanes):
        proj[0:HALO, lanes] = proj[0:HALO, lanes] * first_f
        proj[HALO + 2 * BLOCK :, lanes] = proj[HALO + 2 * BLOCK :, lanes] * last_f

    proj[:, 0:HALF] = proj[:, 0:HALF].astype(BF16).astype(F32)
    ends_off(slice(0, HALF))

    def conv(d, lanes, wlanes):
        total = jnp.broadcast_to(cb_ref[d : d + 1, wlanes], (2 * BLOCK, 128))
        for k in range(4):
            r0 = HALO - 3 + k if d == 0 else HALO + 3 - k
            total = total + cw_ref[d, k : k + 1, wlanes] * proj[pl.ds(r0, 2 * BLOCK), lanes]
        return total * jax.nn.sigmoid(total)

    row_i = lax.broadcasted_iota(jnp.int32, (128, 128), 0)
    lane_i = lax.broadcasted_iota(jnp.int32, (128, 128), 1)
    low = lane_i < HEAD_DIM
    low8 = lax.broadcasted_iota(jnp.int32, (8, 128), 1) < HEAD_DIM
    low1 = lax.broadcasted_iota(jnp.int32, (1, 128), 1) < HEAD_DIM

    def seg_at(v):
        total = jnp.int32(0)
        for m in range(4):
            total = total + jnp.where(marks_ref[0, m] <= v, 1, 0)
        return total

    def pair(value, mask):
        return jnp.where(mask, value[:, 0:1], value[:, 1:2])

    def lanes_of(p):
        return pl.ds(pl.multiple_of(p * 128, 128), 128)

    @pl.loop(0, HALF // 128)
    def _(p):
        wl = pl.ds(pl.multiple_of(core * HALF + p * 128, 128), 128)
        for d in range(2):
            xs[d, :, lanes_of(p)] = conv(d, lanes_of(p), wl).astype(BF16)

    def summary(d, quarter):
        fades_d = [fade_s[d * 2 + d], fade_s[d + 1]]
        for t in range(tq):
            p = quarter * tq + t
            lanes = lanes_of(p)
            inner = slice(t * 128, (t + 1) * 128)
            shift = 128 - 2 * p
            ends, fades = [], []
            for o, j in enumerate((d, 1 - d)):
                n = d * 2 + j
                rows = pl.ds(pl.multiple_of(j * BLOCK, BLOCK), BLOCK)
                tails = pair(pltpu.roll(tail_s[n], shift, 1), low)
                inp = (tails * xs[d, rows, lanes].astype(F32)).astype(BF16)
                ends.append(jnp.dot(bt_s[n], inp, preferred_element_type=F32))
                fades.append(pair(pltpu.roll(fades_d[o], shift, 1), low8)[0:1, :])
            lk[d, :, lanes] = ends[0]
            fb[d, 0:1, lanes] = fades[0]
            ls[d, quarter, :, inner] = (fades[1] * ends[0] + ends[1]).astype(BF16)
            fs[d, quarter, :, inner] = fades[0] * fades[1]

    def level1(ph, d):
        copies = []
        for k in sorted(range(zl), key=lambda k: (k == 0, abs(k - zl // 2))):
            to = lax.rem(q + k, zl)
            summary(d, to)
            if k == 0:
                r1[d, q] = ls[d, q]
                rf1[d, q] = fs[d, q]
                continue
            for a, (src, dst) in enumerate(((ls, r1), (fs, rf1))):
                c = remote(
                    src.at[d, to],
                    dst.at[d, q],
                    l_ss.at[ph, k, a],
                    l_rs.at[ph, k, a],
                    zl_peers[k - 1],
                )
                c.start()
                sent.append(c)
                copies.append(c)
        return copies

    d_a, d_b = yh, 1 - yh
    swap_tile.wait_recv()
    mine, theirs = tile[...].astype(F32), other[...].astype(F32)
    proj[:, HALF : HALF + 128] = jnp.where(core == 0, mine, theirs)
    proj[:, HALF + 128 :] = jnp.where(core == 0, theirs, mine)
    ends_off(slice(HALF, HALF + 128))

    for d in range(2):
        bc = conv(d, slice(HALF, HALF + 128), slice(INNER, INNER + 128))
        pd = par[d : d + 1, :]
        pr = par[2 + d : 3 + d, :]
        pd = jnp.where(core == 0, pd, pltpu.roll(pd, 112, 1))
        pr = jnp.where(core == 0, pr, pltpu.roll(pr, 112, 1))
        tri = (lane_i <= row_i) if d == 0 else (lane_i >= row_i)
        trif = jnp.where(tri, 1.0, 0.0)
        for j in range(2):
            n = d * 2 + j
            t0 = chip * (2 * BLOCK) + j * BLOCK
            st = proj[HALO + j * BLOCK : HALO + (j + 1) * BLOCK, HALF + 128 :]
            st = jnp.where(core == 0, st, pltpu.roll(st, 112, 1))
            pre = st + pd
            step = jnp.maximum(pre, 0.0) + jnp.log1p(jnp.exp(-jnp.abs(pre)))
            rate = -step * pr
            cum = jnp.dot(
                trif, rate, preferred_element_type=F32, precision=lax.Precision.HIGHEST
            )
            cum_s[n] = cum
            cumt_s[n] = cum.T
            stept_s[n] = step.T
            seg_r = jnp.zeros((128, 128), jnp.int32)
            seg_c = jnp.zeros((128, 128), jnp.int32)
            for m in range(4):
                mark = marks_ref[0, m] - t0
                seg_r = seg_r + jnp.where(row_i >= mark, 1, 0)
                seg_c = seg_c + jnp.where(lane_i >= mark, 1, 0)
            in_seg, out_seg = (
                (seg_at(t0 - 1), seg_at(t0 + BLOCK - 1))
                if d == 0
                else (seg_at(t0 + BLOCK), seg_at(t0))
            )
            last = cum[BLOCK - 1 : BLOCK, :] if d == 0 else cum[0:1, :]
            lead_s[n] = jnp.where(seg_r == in_seg, jnp.exp(cum), 0.0)
            tail_s[n] = jnp.where(seg_r == out_seg, jnp.exp(last - cum), 0.0) * step
            same = jnp.where(in_seg == out_seg, 1.0, 0.0)
            fade_s[n, 0:1, :] = jnp.exp(last) * same
            bcj = bc[j * BLOCK : (j + 1) * BLOCK, :]
            b_only = jnp.where(low, bcj, 0.0).astype(BF16)
            c_low = pltpu.roll(bcj, HEAD_DIM, 1).astype(BF16)
            scores = lax.dot_general(
                c_low, b_only, (((1,), (1,)), ((), ())), preferred_element_type=F32
            )
            msc_s[n] = jnp.where(tri & (seg_r == seg_c), scores, 0.0)
            bt_s[n] = bcj.T[0:STATE, :].astype(BF16)
            cr_s[n] = c_low

    in1a = level1(0, d_a)
    in1b = level1(1, d_b)

    def local_pairs(lo, hi):
        @pl.loop(lo, hi)
        def _(p):
            lanes = lanes_of(p)
            shift = 128 - 2 * p
            head = core * (HEADS // 2) + 2 * p
            for d in range(2):
                skips = jnp.where(low1, skip_ref[d, head], skip_ref[d, head + 1])
                for j in range(2):
                    n = d * 2 + j
                    rows = slice(j * BLOCK, (j + 1) * BLOCK)
                    xt = xs[d, rows, lanes]
                    cums = pltpu.roll(cum_s[n], shift, 1)
                    ws = []
                    for hh in range(2):
                        h = pl.ds(2 * p + hh, 1)
                        gap = jnp.minimum(cums[:, hh : hh + 1] - cumt_s[n, h, :], 0.0)
                        ws.append((jnp.exp(gap) * msc_s[n] * stept_s[n, h, :]).astype(BF16))
                    xf = xt.astype(F32)
                    xl = jnp.where(low, xf, 0.0).astype(BF16)
                    xh = jnp.where(low, 0.0, xf).astype(BF16)
                    inner = jnp.dot(
                        jnp.concatenate(ws, axis=1),
                        jnp.concatenate([xl, xh], axis=0),
                        preferred_element_type=F32,
                    )
                    ys[d, rows, lanes] = inner + skips * xf

    def member(d, step, count):
        return d * (count - 1) + (1 - 2 * d) * step

    def level2(ph, d, copies):
        for c in copies:
            c.wait_recv()
        total = jnp.zeros((STATE, ql), F32)
        fade = jnp.ones((1, ql), F32)
        for step in range(zl):
            c = member(d, step, zl)
            f = rf1[d, c]
            total = f * total + r1[d, c].astype(F32)
            fade = fade * f
        gb[d, zh] = total.astype(BF16)
        gf[d, zh] = fade
        out = []
        for k in range(1, zh_n):
            for a, buf in enumerate((gb, gf)):
                c = remote(
                    buf.at[d, zh],
                    buf.at[d, zh],
                    g_ss.at[ph, k, a],
                    g_rs.at[ph, k, a],
                    zh_peers[k - 1],
                )
                c.start()
                sent.append(c)
                out.append(c)
        return out

    def level4(ph, d, state):
        for step in range(zh_n - 1):
            c = member(d, step, zh_n)
            before = (1 - 2 * d) * (zh - c) > 0
            longer = gf[d, c] * state + gb[d, c].astype(F32)
            state = jnp.where(before, longer, state)
        for step in range(zl):
            c = member(d, step, zl)
            o4[d, c] = state.astype(BF16)
            if step < zl - 1:
                state = rf1[d, c] * state + r1[d, c].astype(F32)
        out = []
        for k in range(1, zl):
            to = lax.rem(q + k, zl)
            c = remote(
                o4.at[d, to], sin.at[d, q], l_ss.at[ph, 0, k], l_rs.at[ph, 0, k], zl_peers[k - 1]
            )
            c.start()
            sent.append(c)
            out.append(c)
        sin[d, q] = o4[d, q]
        return out

    local_pairs(0, 4)
    in2a = level2(0, d_a, in1a)
    local_pairs(4, 7)
    in2b = level2(1, d_b, in1b)
    local_pairs(7, 8)
    for c in in2a:
        c.wait_recv()
    total = jnp.zeros((STATE, ql), F32)
    for step in range(zh_n):
        c = member(d_a, step, zh_n)
        total = gf[d_a, c] * total + gb[d_a, c].astype(F32)
    tb[...] = total.astype(BF16)
    in3 = remote(tb, tr, g_ss.at[0, 0, 0], g_rs.at[0, 0, 0], y_peer)
    in3.start()
    sent.append(in3)
    in4a = level4(0, d_a, jnp.zeros((STATE, ql), F32))
    for c in in2b:
        c.wait_recv()
    in3.wait_recv()
    in4b = level4(1, d_b, tr[...].astype(F32))

    row_q = lax.div(lax.broadcasted_iota(jnp.int32, (ql, ql), 0), HEAD_DIM)
    lane_q = lax.div(lax.broadcasted_iota(jnp.int32, (ql, ql), 1), HEAD_DIM)
    ones = jnp.where(row_q == lane_q, 1.0 / HEAD_DIM, 0.0).astype(BF16)

    def finish(quarter, d, last):
        lanes = pl.ds(pl.multiple_of(quarter * ql, ql), ql)
        wl = pl.ds(pl.multiple_of(core * HALF + quarter * ql, ql), ql)
        gains = jnp.where(d == 0, gain_ref[0:1, wl], gain_ref[1:2, wl])
        entering = sin[d, quarter]
        second = fb[d, 0:1, lanes] * entering.astype(F32) + lk[d, :, lanes]
        for j, state in ((d, entering), (1 - d, second.astype(BF16))):
            n = d * 2 + j
            rows = pl.ds(pl.multiple_of(j * BLOCK, BLOCK), BLOCK)
            carried = jnp.dot(cr_s[n, :, 0:STATE], state, preferred_element_type=F32)
            lead = pltpu.roll(lead_s[n], 128 - 2 * tq * quarter, 1)
            leads = jnp.concatenate(
                [
                    jnp.where(low, lead[:, 2 * t : 2 * t + 1], lead[:, 2 * t + 1 : 2 * t + 2])
                    for t in range(tq)
                ],
                axis=1,
            )
            yv = ys[d, rows, lanes] + leads * carried
            mean = jnp.dot((yv * yv).astype(BF16), ones, preferred_element_type=F32)
            res = yv * lax.rsqrt(mean + 1e-05) * gains
            if last:
                outb[quarter, j] = (res + ys[1 - d, rows, lanes]).astype(BF16)
            else:
                ys[d, rows, lanes] = res

    finish(q, d_a, False)
    for k in range(1, zl):
        in4a[k - 1].wait_recv()
        finish(lax.rem(q + zl - k, zl), d_a, False)
    outs = []
    for k in range(zl):
        quarter = lax.rem(q + zl - k, zl)
        if k > 0:
            in4b[k - 1].wait_recv()
        finish(quarter, d_b, True)
        cols = pl.ds(pl.multiple_of(core * HALF + quarter * ql, ql), ql)
        oc = remote(
            outb.at[quarter, 1 - core], out_ref.at[0, :, cols], o_ss.at[k], o_rs.at[k], partner
        )
        oc.start()
        own = pltpu.make_async_copy(
            outb.at[quarter, core], out_ref.at[0, :, cols], own_sem.at[k]
        )
        own.start()
        outs.append((oc, own))
    for oc, own in outs:
        own.wait()
        oc.wait()
    for c in sent:
        c.wait_send()


def solution(mesh):
    nx, ny, seqs = mesh.shape["fsdp"], mesh.shape["batch"], mesh.shape["seq"]
    nz = seqs // 4
    zl = 4 if nz % 4 == 0 and nz > 4 else 2
    zh_n = nz // zl
    ql = HALF // zl
    cfg = (nx, ny, nz, zl, zh_n, seqs)

    def on_device(hidden, in_weight, marks, cw, cb, dtb, dec, skip, gain):
        kb = in_weight.shape[0]
        vmem = pl.BlockSpec(memory_space=pltpu.VMEM)
        hbm = pl.BlockSpec(memory_space=pl.ANY)
        smem = pl.BlockSpec(memory_space=pltpu.SMEM)
        dma = pltpu.SemaphoreType.DMA
        return pl.pallas_call(
            functools.partial(kernel, cfg),
            out_shape=jax.ShapeDtypeStruct(hidden.shape, BF16),
            in_specs=[hbm, hbm, smem, vmem, vmem, vmem, vmem, smem, vmem],
            out_specs=hbm,
            scratch_shapes=[
                pltpu.VMEM((nx, ny, 3 * PART, kb), BF16),
                pltpu.VMEM((ROWS, INNER), BF16),
                pltpu.VMEM((ROWS, HALF + 256), F32),
                pltpu.VMEM((ROWS, 128), BF16),
                pltpu.VMEM((ROWS, 128), BF16),
                pltpu.VMEM((2, 2 * BLOCK, HALF), BF16),
                pltpu.VMEM((2, 2 * BLOCK, HALF), F32),
                pltpu.VMEM((2, STATE, HALF), F32),
                pltpu.VMEM((2, zl, STATE, ql), BF16),
                pltpu.VMEM((2, zl, 1, ql), F32),
                pltpu.VMEM((2, 8, HALF), F32),
                pltpu.VMEM((2, zl, STATE, ql), BF16),
                pltpu.VMEM((2, zl, 1, ql), F32),
                pltpu.VMEM((2, zh_n, STATE, ql), BF16),
                pltpu.VMEM((2, zh_n, 1, ql), F32),
                pltpu.VMEM((STATE, ql), BF16),
                pltpu.VMEM((STATE, ql), BF16),
                pltpu.VMEM((2, zl, STATE, ql), BF16),
                pltpu.VMEM((2, zl, STATE, ql), BF16),
                pltpu.VMEM((zl, 2, BLOCK, ql), BF16),
                pltpu.VMEM((8, 128), F32),
                pltpu.VMEM((4, 128, 128), F32),
                pltpu.VMEM((4, 128, 128), F32),
                pltpu.VMEM((4, 128, 128), F32),
                pltpu.VMEM((4, 128, 128), F32),
                pltpu.VMEM((4, 128, 128), F32),
                pltpu.VMEM((4, 128, 128), F32),
                pltpu.VMEM((4, STATE, 128), BF16),
                pltpu.VMEM((4, 128, 128), BF16),
                pltpu.VMEM((4, 8, 128), F32),
                dma((64,)),
                dma((64,)),
                dma((4,)),
                dma((4,)),
                dma((2, 4, 4)),
                dma((2, 4, 4)),
                dma((2, 3, 2)),
                dma((2, 3, 2)),
                dma((6,)),
                dma((4,)),
                dma((4,)),
                dma((4,)),
            ],
            compiler_params=pltpu.CompilerParams(
                collective_id=0, has_side_effects=True, vmem_limit_bytes=48 * 1024 * 1024
            ),
        )(hidden, in_weight.T, marks, cw, cb, dtb, dec, skip, gain)

    group = P(("fsdp", "batch"), "seq", None)
    rows = P(("fsdp", "batch"), None)
    return jax.shard_map(
        on_device,
        mesh=mesh,
        in_specs=(group, rows, rows, P(), P(), P(), P(), P(), P()),
        out_specs=group,
        check_vma=False,
    )
```

```python
import functools

import jax
import jax.numpy as jnp
from jax import lax
from jax.experimental import pallas as pl
from jax.experimental.pallas import tpu as pltpu
from jax.sharding import PartitionSpec as P

MESH = pl.DeviceIdType.MESH
HEADS = 32
HEAD_DIM = 64
STATE = 64
BLOCK = 128
INNER = 2048
HALF = 1024
PART = 384
HALO = 16
ROWS = 2 * BLOCK + 2 * HALO
F32 = jnp.float32
BF16 = jnp.bfloat16


def kernel(
    cfg,
    hid_ref,
    w_ref,
    marks_in,
    cw_in,
    cb_in,
    dtb_in,
    dec_in,
    skip_in,
    gain_in,
    out_ref,
    marks_ref,
    cw_ref,
    cb_ref,
    dtb_ref,
    dec_ref,
    skip_ref,
    gain_ref,
    wb,
    hidb,
    proj,
    tile,
    other,
    xs,
    ys,
    lk,
    ls,
    fs,
    fb,
    r1,
    rf1,
    gb,
    gf,
    tb,
    tr,
    o4,
    sin,
    outb,
    par,
    cum_s,
    cumt_s,
    stept_s,
    tail_s,
    lead_s,
    msc_s,
    bt_s,
    cr_s,
    fade_s,
    w_ss,
    w_rs,
    h_ss,
    h_rs,
    l_ss,
    l_rs,
    g_ss,
    g_rs,
    in_sem,
    o_ss,
    o_rs,
    own_sem,
):
    nx, ny, nz, zl, zh_n, seqs = cfg
    ql = HALF // zl
    tq = ql // 128
    s = lax.axis_index("seq")
    x = lax.axis_index("fsdp")
    y = lax.axis_index("batch")
    core = lax.rem(s, 2)
    chip = lax.div(s, 2)
    chips = seqs // 2
    z = lax.rem(chip, nz)
    yh = lax.div(chip, nz)
    q = lax.rem(z, zl)
    zh = lax.div(z, zl)

    def dev(seq, xx=x, yy=y):
        return {"seq": seq, "fsdp": xx, "batch": yy}

    def at_z(zz):
        return dev((yh * nz + zz) * 2 + core)

    partner = dev(chip * 2 + 1 - core)
    xp, xm = dev(s, lax.rem(x + 1, nx)), dev(s, lax.rem(x + nx - 1, nx))
    wrap_p = lax.div(y + 1, ny)
    wrap_m = 1 - lax.div(y + ny - 1, ny)
    yp = dev(lax.rem(s + (seqs // 2) * wrap_p, seqs), x, lax.rem(y + 1, ny))
    ym = dev(lax.rem(s + (seqs // 2) * wrap_m, seqs), x, lax.rem(y + ny - 1, ny))
    nxt = lax.rem(chip + 1, chips)
    prv = lax.rem(chip + chips - 1, chips)
    rot = lax.rem(z, 3) if nx > 1 else jnp.int32(0)
    zp, zm = at_z(lax.rem(z + 1, nz)), at_z(lax.rem(z + nz - 1, nz))
    zl_peers = [at_z(zh * zl + lax.rem(q + k, zl)) for k in range(1, zl)]
    zh_peers = [at_z(lax.rem(zh + k, zh_n) * zl + q) for k in range(1, zh_n)]
    y_peer = dev(((1 - yh) * nz + z) * 2 + core)

    barrier = pltpu.get_barrier_semaphore()
    greet = [partner, dev(nxt * 2), dev(nxt * 2 + 1), dev(prv * 2), dev(prv * 2 + 1)]
    greet += zl_peers + zh_peers + [y_peer]
    if nx > 1:
        greet += [xp, xm, yp, ym, zp, zm]
    for peer in greet:
        pl.semaphore_signal(barrier, inc=1, device_id=peer, device_id_type=MESH)

    own_rows = pl.ds(pl.multiple_of(HALO + core * BLOCK, HALO), BLOCK)
    kb = w_ref.shape[1]
    reads = [(hid_ref.at[0], hidb.at[own_rows, :])]
    part_lanes = [
        pl.ds(pl.multiple_of(lax.rem(rot + u, 3) * PART, PART), PART) for u in (1, 2, 0)
    ]
    bases = [lax.rem(p + 5 - rot, 3) * PART for p in range(3)]
    cols0 = core * HALF
    for src, dst, count in (
        (cols0, bases[0], PART),
        (cols0 + PART, bases[1], PART),
        (cols0 + 2 * PART, bases[2], 256),
        (INNER + 128 * core, bases[2] + 256, 32),
        (INNER + 32, bases[2] + 288, 96),
    ):
        reads.append(
            (
                w_ref.at[pl.ds(pl.multiple_of(src, 32), count), :],
                wb.at[0, 0, pl.ds(pl.multiple_of(dst, 32), count), :],
            )
        )
    early = len(reads)
    reads += [
        (marks_in, marks_ref),
        (cw_in, cw_ref),
        (cb_in, cb_ref),
        (dtb_in, dtb_ref),
        (dec_in, dec_ref),
        (skip_in, skip_ref),
        (gain_in, gain_ref),
    ]
    reads = [pltpu.make_async_copy(a, b, in_sem.at[k]) for k, (a, b) in enumerate(reads)]
    for c in reads:
        c.start()
    par[...] = jnp.zeros_like(par)
    fade_s[...] = jnp.zeros_like(fade_s)
    for c in reads[1:early]:
        c.wait()
    pl.semaphore_wait(barrier, len(greet))

    def remote(src, dst, ssem, rsem, peer):
        return pltpu.make_async_remote_copy(
            src_ref=src,
            dst_ref=dst,
            send_sem=ssem,
            recv_sem=rsem,
            device_id=peer,
            device_id_type=MESH,
        )

    sent = []

    msgs = {}
    zmsgs = {}

    def w_send(half, a, b, r0, n, axis, step, tag):
        swap = half == 1
        dim_x = (axis == 1) != swap
        i, j = (b, a) if swap else (a, b)
        ii = (i + step) % nx if dim_x else i
        jj = j if dim_x else (j + step) % ny
        peer = (xp if step > 0 else xm) if dim_x else (yp if step > 0 else ym)
        k = len(msgs)
        rows = pl.ds(half * PART + r0, n)
        copy = remote(
            wb.at[i, j, rows, :], wb.at[ii, jj, rows, :], w_ss.at[k], w_rs.at[k], peer
        )
        copy.start()
        sent.append(copy)
        aa, bb = (jj, ii) if swap else (ii, jj)
        msgs[(half, aa, bb, tag)] = copy

    def w_wait(half, a, b):
        for tag in range(2):
            if (half, a, b, tag) in msgs:
                msgs[(half, a, b, tag)].wait_recv()
        i, j = (b, a) if half == 1 else (a, b)
        k = 32 + len(zmsgs)
        copy = remote(
            wb.at[i, j, pl.ds(half * (PART + hk // 2), hk // 2), :],
            wb.at[i, j, pl.ds(2 * PART + half * (hk // 2), hk // 2), :],
            w_ss.at[k],
            w_rs.at[k],
            zm if half else zp,
        )
        copy.start()
        sent.append(copy)
        zmsgs[(half, i, j)] = copy

    hk = PART
    halves = (0, 1)
    if nx > 1:
        for h in halves:
            w_send(h, 0, 0, 0, hk, 1, 1, 0)
            w_send(h, 0, 0, 0, hk, 1, -1, 0)

    pc = remote(hid_ref.at[0], hidb.at[own_rows, :], h_ss.at[0], h_rs.at[0], partner)
    pc.start()
    sent.append(pc)
    target = core * nxt + (1 - core) * prv
    src_rows = pl.ds(pl.multiple_of((BLOCK - HALO) * core, HALO), HALO)
    dst_rows = pl.ds(pl.multiple_of((HALO + 2 * BLOCK) * (1 - core), HALO), HALO)
    for c in range(2):
        copy = remote(
            hid_ref.at[0, src_rows, :],
            hidb.at[dst_rows, :],
            h_ss.at[1 + c],
            h_rs.at[2 - core],
            dev(target * 2 + c),
        )
        copy.start()
        sent.append(copy)

    def rows_wait():
        reads[0].wait()
        for c in reads[early:]:
            c.wait()
        par[0:2, 0:HEADS] = dtb_ref[...]
        par[2:4, 0:HEADS] = dec_ref[...]
        pc.wait_recv()
        for side in range(2):
            rows = pl.ds((HALO + 2 * BLOCK) * side, HALO)
            remote(
                hid_ref.at[0, 0:HALO, :], hidb.at[rows, :], h_ss.at[1], h_rs.at[1 + side], partner
            ).wait_recv()

    def project(slots, parts, first=False):
        left = []
        for i, j in slots:
            k = lax.rem(x + nx - i, nx) * ny + lax.rem(y + ny - j, ny)
            left.append(hidb[:, pl.ds(pl.multiple_of(k * kb, kb), kb)])
        left = jnp.concatenate(left, axis=1)
        for u in parts:
            rows = slice(u * PART, (u + 1) * PART)
            right = jnp.concatenate([wb[i, j, rows, :] for i, j in slots], axis=1)
            value = lax.dot_general(
                left, right, (((1,), (1,)), ((), ())), preferred_element_type=F32
            )
            if first:
                proj[:, part_lanes[u]] = value
            else:
                proj[:, part_lanes[u]] += value

    if nx > 1:
        xy, zz = (0, 1), (2,)
        order_k = (
            ((0, 0), (0, 1)),
            ((1, 0), (0, 3)),
            ((3, 0), (1, 1)),
            ((3, 3), (1, 3)),
            ((3, 1), (0, 2)),
            ((2, 0), (2, 1)),
            ((1, 2), (3, 2)),
            ((2, 3), (2, 2)),
        )
        for h in halves:
            w_send(h, 0, 0, 0, hk, 2, 1, 0)
            w_send(h, 0, 0, 0, hk, 2, -1, 0)
        for h in halves:
            w_wait(h, 1, 0)
            w_send(h, 1, 0, 0, hk // 2, 1, 1, 0)
            w_wait(h, 3, 0)
            w_send(h, 3, 0, hk // 2, hk // 2, 1, -1, 1)
        for h in halves:
            for a in (1, 3):
                w_send(h, a, 0, 0, hk, 2, 1, 0)
                w_send(h, a, 0, 0, hk, 2, -1, 0)
        rows_wait()
        for h in halves:
            w_wait(h, 0, 1)
            w_send(h, 0, 1, 0, hk, 2, 1, 0)
            w_wait(h, 0, 3)
        project(order_k[0], xy, True)
        for h in halves:
            w_wait(h, 2, 0)
            w_send(h, 2, 0, 0, hk, 2, 1, 0)
            w_send(h, 2, 0, 0, hk, 2, -1, 0)
        project(order_k[1], xy)
        for h in halves:
            w_wait(h, 1, 1)
            w_send(h, 1, 1, 0, hk, 2, 1, 0)
            w_wait(h, 3, 3)
            w_send(h, 3, 3, 0, hk, 2, -1, 0)
        project(order_k[2], xy)
        for h in halves:
            w_wait(h, 1, 3)
            w_wait(h, 3, 1)
        project(order_k[3], xy)
        for h in halves:
            w_wait(h, 2, 3)
            w_send(h, 2, 3, 0, hk, 2, -1, 0)
            w_wait(h, 0, 2)
        project(order_k[4], xy)
        for h in halves:
            w_wait(h, 2, 1)
            w_wait(h, 1, 2)
        project(order_k[5], xy)

        def z_wait(slots):
            for i, j in slots:
                for h in halves:
                    if (i, j) != (0, 0):
                        zmsgs[(h, i, j)].wait_recv()

        z_wait(order_k[0])
        project(order_k[0], zz, True)
        z_wait(order_k[1])
        project(order_k[1], zz)
        for h in halves:
            w_wait(h, 3, 2)
        project(order_k[6], xy)
        for h in halves:
            w_wait(h, 2, 2)
        project(order_k[7], xy)
        for slots in order_k[2:]:
            z_wait(slots)
            project(slots, zz)
    else:
        rows_wait()
        project(((0, 0),), (0, 1, 2), True)

    tile[...] = proj[:, HALF : HALF + 128].astype(BF16)
    swap_tile = remote(tile, other, h_ss.at[3], h_rs.at[3], partner)
    swap_tile.start()
    sent.append(swap_tile)
    first_f = jnp.where(chip == 0, 0.0, 1.0)
    last_f = jnp.where(chip == chips - 1, 0.0, 1.0)

    def ends_off(lanes):
        proj[0:HALO, lanes] = proj[0:HALO, lanes] * first_f
        proj[HALO + 2 * BLOCK :, lanes] = proj[HALO + 2 * BLOCK :, lanes] * last_f

    proj[:, 0:HALF] = proj[:, 0:HALF].astype(BF16).astype(F32)
    ends_off(slice(0, HALF))

    def conv(d, lanes, wlanes):
        total = jnp.broadcast_to(cb_ref[d : d + 1, wlanes], (2 * BLOCK, 128))
        for k in range(4):
            r0 = HALO - 3 + k if d == 0 else HALO + 3 - k
            total = total + cw_ref[d, k : k + 1, wlanes] * proj[pl.ds(r0, 2 * BLOCK), lanes]
        return total * jax.nn.sigmoid(total)

    row_i = lax.broadcasted_iota(jnp.int32, (128, 128), 0)
    lane_i = lax.broadcasted_iota(jnp.int32, (128, 128), 1)
    low = lane_i < HEAD_DIM
    low8 = lax.broadcasted_iota(jnp.int32, (8, 128), 1) < HEAD_DIM
    low1 = lax.broadcasted_iota(jnp.int32, (1, 128), 1) < HEAD_DIM

    def seg_at(v):
        total = jnp.int32(0)
        for m in range(4):
            total = total + jnp.where(marks_ref[0, m] <= v, 1, 0)
        return total

    def pair(value, mask):
        return jnp.where(mask, value[:, 0:1], value[:, 1:2])

    def lanes_of(p):
        return pl.ds(pl.multiple_of(p * 128, 128), 128)

    @pl.loop(0, HALF // 128)
    def _(p):
        wl = pl.ds(pl.multiple_of(core * HALF + p * 128, 128), 128)
        for d in range(2):
            xs[d, :, lanes_of(p)] = conv(d, lanes_of(p), wl).astype(BF16)

    def summary(d, quarter):
        fades_d = [fade_s[d * 2 + d], fade_s[d + 1]]
        for t in range(tq):
            p = quarter * tq + t
            lanes = lanes_of(p)
            inner = slice(t * 128, (t + 1) * 128)
            shift = 128 - 2 * p
            ends, fades = [], []
            for o, j in enumerate((d, 1 - d)):
                n = d * 2 + j
                rows = pl.ds(pl.multiple_of(j * BLOCK, BLOCK), BLOCK)
                tails = pair(pltpu.roll(tail_s[n], shift, 1), low)
                inp = (tails * xs[d, rows, lanes].astype(F32)).astype(BF16)
                ends.append(jnp.dot(bt_s[n], inp, preferred_element_type=F32))
                fades.append(pair(pltpu.roll(fades_d[o], shift, 1), low8)[0:1, :])
            lk[d, :, lanes] = ends[0]
            fb[d, 0:1, lanes] = fades[0]
            ls[d, quarter, :, inner] = (fades[1] * ends[0] + ends[1]).astype(BF16)
            fs[d, quarter, :, inner] = fades[0] * fades[1]

    def level1(ph, d):
        copies = []
        for k in sorted(range(zl), key=lambda k: (k == 0, abs(k - zl // 2))):
            to = lax.rem(q + k, zl)
            summary(d, to)
            if k == 0:
                r1[d, q] = ls[d, q]
                rf1[d, q] = fs[d, q]
                continue
            for a, (src, dst) in enumerate(((ls, r1), (fs, rf1))):
                c = remote(
                    src.at[d, to],
                    dst.at[d, q],
                    l_ss.at[ph, k, a],
                    l_rs.at[ph, k, a],
                    zl_peers[k - 1],
                )
                c.start()
                sent.append(c)
                copies.append(c)
        return copies

    d_a, d_b = yh, 1 - yh
    swap_tile.wait_recv()
    mine, theirs = tile[...].astype(F32), other[...].astype(F32)
    proj[:, HALF : HALF + 128] = jnp.where(core == 0, mine, theirs)
    proj[:, HALF + 128 :] = jnp.where(core == 0, theirs, mine)
    ends_off(slice(HALF, HALF + 128))

    for d in range(2):
        bc = conv(d, slice(HALF, HALF + 128), slice(INNER, INNER + 128))
        pd = par[d : d + 1, :]
        pr = par[2 + d : 3 + d, :]
        pd = jnp.where(core == 0, pd, pltpu.roll(pd, 112, 1))
        pr = jnp.where(core == 0, pr, pltpu.roll(pr, 112, 1))
        tri = (lane_i <= row_i) if d == 0 else (lane_i >= row_i)
        trif = jnp.where(tri, 1.0, 0.0)
        for j in range(2):
            n = d * 2 + j
            t0 = chip * (2 * BLOCK) + j * BLOCK
            st = proj[HALO + j * BLOCK : HALO + (j + 1) * BLOCK, HALF + 128 :]
            st = jnp.where(core == 0, st, pltpu.roll(st, 112, 1))
            pre = st + pd
            step = jnp.maximum(pre, 0.0) + jnp.log1p(jnp.exp(-jnp.abs(pre)))
            rate = -step * pr
            cum = jnp.dot(
                trif, rate, preferred_element_type=F32, precision=lax.Precision.HIGHEST
            )
            cum_s[n] = cum
            cumt_s[n] = cum.T
            stept_s[n] = step.T
            seg_r = jnp.zeros((128, 128), jnp.int32)
            seg_c = jnp.zeros((128, 128), jnp.int32)
            for m in range(4):
                mark = marks_ref[0, m] - t0
                seg_r = seg_r + jnp.where(row_i >= mark, 1, 0)
                seg_c = seg_c + jnp.where(lane_i >= mark, 1, 0)
            in_seg, out_seg = (
                (seg_at(t0 - 1), seg_at(t0 + BLOCK - 1))
                if d == 0
                else (seg_at(t0 + BLOCK), seg_at(t0))
            )
            last = cum[BLOCK - 1 : BLOCK, :] if d == 0 else cum[0:1, :]
            lead_s[n] = jnp.where(seg_r == in_seg, jnp.exp(cum), 0.0)
            tail_s[n] = jnp.where(seg_r == out_seg, jnp.exp(last - cum), 0.0) * step
            same = jnp.where(in_seg == out_seg, 1.0, 0.0)
            fade_s[n, 0:1, :] = jnp.exp(last) * same
            bcj = bc[j * BLOCK : (j + 1) * BLOCK, :]
            b_only = jnp.where(low, bcj, 0.0).astype(BF16)
            c_low = pltpu.roll(bcj, HEAD_DIM, 1).astype(BF16)
            scores = lax.dot_general(
                c_low, b_only, (((1,), (1,)), ((), ())), preferred_element_type=F32
            )
            msc_s[n] = jnp.where(tri & (seg_r == seg_c), scores, 0.0)
            bt_s[n] = bcj.T[0:STATE, :].astype(BF16)
            cr_s[n] = c_low

    in1a = level1(0, d_a)
    in1b = level1(1, d_b)

    def local_pairs(lo, hi):
        @pl.loop(lo, hi)
        def _(p):
            lanes = lanes_of(p)
            shift = 128 - 2 * p
            head = core * (HEADS // 2) + 2 * p
            for d in range(2):
                skips = jnp.where(low1, skip_ref[d, head], skip_ref[d, head + 1])
                for j in range(2):
                    n = d * 2 + j
                    rows = slice(j * BLOCK, (j + 1) * BLOCK)
                    xt = xs[d, rows, lanes]
                    cums = pltpu.roll(cum_s[n], shift, 1)
                    ws = []
                    for hh in range(2):
                        h = pl.ds(2 * p + hh, 1)
                        gap = jnp.minimum(cums[:, hh : hh + 1] - cumt_s[n, h, :], 0.0)
                        ws.append((jnp.exp(gap) * msc_s[n] * stept_s[n, h, :]).astype(BF16))
                    xf = xt.astype(F32)
                    xl = jnp.where(low, xf, 0.0).astype(BF16)
                    xh = jnp.where(low, 0.0, xf).astype(BF16)
                    inner = jnp.dot(
                        jnp.concatenate(ws, axis=1),
                        jnp.concatenate([xl, xh], axis=0),
                        preferred_element_type=F32,
                    )
                    ys[d, rows, lanes] = inner + skips * xf

    def member(d, step, count):
        return d * (count - 1) + (1 - 2 * d) * step

    def level2(ph, d, copies):
        for c in copies:
            c.wait_recv()
        total = jnp.zeros((STATE, ql), F32)
        fade = jnp.ones((1, ql), F32)
        for step in range(zl):
            c = member(d, step, zl)
            f = rf1[d, c]
            total = f * total + r1[d, c].astype(F32)
            fade = fade * f
        gb[d, zh] = total.astype(BF16)
        gf[d, zh] = fade
        out = []
        for k in range(1, zh_n):
            for a, buf in enumerate((gb, gf)):
                c = remote(
                    buf.at[d, zh],
                    buf.at[d, zh],
                    g_ss.at[ph, k, a],
                    g_rs.at[ph, k, a],
                    zh_peers[k - 1],
                )
                c.start()
                sent.append(c)
                out.append(c)
        return out

    def level4(ph, d, state):
        for step in range(zh_n - 1):
            c = member(d, step, zh_n)
            before = (1 - 2 * d) * (zh - c) > 0
            longer = gf[d, c] * state + gb[d, c].astype(F32)
            state = jnp.where(before, longer, state)
        for step in range(zl):
            c = member(d, step, zl)
            o4[d, c] = state.astype(BF16)
            if step < zl - 1:
                state = rf1[d, c] * state + r1[d, c].astype(F32)
        out = []
        for k in range(1, zl):
            to = lax.rem(q + k, zl)
            c = remote(
                o4.at[d, to], sin.at[d, q], l_ss.at[ph, 0, k], l_rs.at[ph, 0, k], zl_peers[k - 1]
            )
            c.start()
            sent.append(c)
            out.append(c)
        sin[d, q] = o4[d, q]
        return out

    local_pairs(0, 4)
    in2a = level2(0, d_a, in1a)
    local_pairs(4, 7)
    in2b = level2(1, d_b, in1b)
    local_pairs(7, 8)
    for c in in2a:
        c.wait_recv()
    total = jnp.zeros((STATE, ql), F32)
    for step in range(zh_n):
        c = member(d_a, step, zh_n)
        total = gf[d_a, c] * total + gb[d_a, c].astype(F32)
    tb[...] = total.astype(BF16)
    in3 = remote(tb, tr, g_ss.at[0, 0, 0], g_rs.at[0, 0, 0], y_peer)
    in3.start()
    sent.append(in3)
    in4a = level4(0, d_a, jnp.zeros((STATE, ql), F32))
    for c in in2b:
        c.wait_recv()
    in3.wait_recv()
    in4b = level4(1, d_b, tr[...].astype(F32))

    row_q = lax.div(lax.broadcasted_iota(jnp.int32, (ql, ql), 0), HEAD_DIM)
    lane_q = lax.div(lax.broadcasted_iota(jnp.int32, (ql, ql), 1), HEAD_DIM)
    ones = jnp.where(row_q == lane_q, 1.0 / HEAD_DIM, 0.0).astype(BF16)

    def finish(quarter, d, last):
        lanes = pl.ds(pl.multiple_of(quarter * ql, ql), ql)
        wl = pl.ds(pl.multiple_of(core * HALF + quarter * ql, ql), ql)
        gains = jnp.where(d == 0, gain_ref[0:1, wl], gain_ref[1:2, wl])
        entering = sin[d, quarter]
        second = fb[d, 0:1, lanes] * entering.astype(F32) + lk[d, :, lanes]
        for j, state in ((d, entering), (1 - d, second.astype(BF16))):
            n = d * 2 + j
            rows = pl.ds(pl.multiple_of(j * BLOCK, BLOCK), BLOCK)
            carried = jnp.dot(cr_s[n, :, 0:STATE], state, preferred_element_type=F32)
            lead = pltpu.roll(lead_s[n], 128 - 2 * tq * quarter, 1)
            leads = jnp.concatenate(
                [
                    jnp.where(low, lead[:, 2 * t : 2 * t + 1], lead[:, 2 * t + 1 : 2 * t + 2])
                    for t in range(tq)
                ],
                axis=1,
            )
            yv = ys[d, rows, lanes] + leads * carried
            mean = jnp.dot((yv * yv).astype(BF16), ones, preferred_element_type=F32)
            res = yv * lax.rsqrt(mean + 1e-05) * gains
            if last:
                outb[quarter, j] = (res + ys[1 - d, rows, lanes]).astype(BF16)
            else:
                ys[d, rows, lanes] = res

    finish(q, d_a, False)
    for k in range(1, zl):
        in4a[k - 1].wait_recv()
        finish(lax.rem(q + zl - k, zl), d_a, False)
    outs = []
    for k in range(zl):
        quarter = lax.rem(q + zl - k, zl)
        if k > 0:
            in4b[k - 1].wait_recv()
        finish(quarter, d_b, True)
        cols = pl.ds(pl.multiple_of(core * HALF + quarter * ql, ql), ql)
        oc = remote(
            outb.at[quarter, 1 - core], out_ref.at[0, :, cols], o_ss.at[k], o_rs.at[k], partner
        )
        oc.start()
        own = pltpu.make_async_copy(
            outb.at[quarter, core], out_ref.at[0, :, cols], own_sem.at[k]
        )
        own.start()
        outs.append((oc, own))
    for oc, own in outs:
        own.wait()
        oc.wait()
    for c in sent:
        c.wait_send()


def solution(mesh):
    nx, ny, seqs = mesh.shape["fsdp"], mesh.shape["batch"], mesh.shape["seq"]
    nz = seqs // 4
    zl = 4 if nz % 4 == 0 and nz > 4 else 2
    zh_n = nz // zl
    ql = HALF // zl
    cfg = (nx, ny, nz, zl, zh_n, seqs)

    def on_device(hidden, in_weight, marks, cw, cb, dtb, dec, skip, gain):
        kb = in_weight.shape[0]
        hbm = pl.BlockSpec(memory_space=pl.ANY)
        dma = pltpu.SemaphoreType.DMA
        return pl.pallas_call(
            functools.partial(kernel, cfg),
            out_shape=jax.ShapeDtypeStruct(hidden.shape, BF16),
            in_specs=[hbm] * 9,
            out_specs=hbm,
            scratch_shapes=[
                pltpu.SMEM(marks.shape, jnp.int32),
                pltpu.VMEM(cw.shape, F32),
                pltpu.VMEM(cb.shape, F32),
                pltpu.VMEM(dtb.shape, F32),
                pltpu.VMEM(dec.shape, F32),
                pltpu.SMEM(skip.shape, F32),
                pltpu.VMEM(gain.shape, F32),
                pltpu.VMEM((nx, ny, 3 * PART, kb), BF16),
                pltpu.VMEM((ROWS, INNER), BF16),
                pltpu.VMEM((ROWS, HALF + 256), F32),
                pltpu.VMEM((ROWS, 128), BF16),
                pltpu.VMEM((ROWS, 128), BF16),
                pltpu.VMEM((2, 2 * BLOCK, HALF), BF16),
                pltpu.VMEM((2, 2 * BLOCK, HALF), F32),
                pltpu.VMEM((2, STATE, HALF), F32),
                pltpu.VMEM((2, zl, STATE, ql), BF16),
                pltpu.VMEM((2, zl, 1, ql), F32),
                pltpu.VMEM((2, 8, HALF), F32),
                pltpu.VMEM((2, zl, STATE, ql), BF16),
                pltpu.VMEM((2, zl, 1, ql), F32),
                pltpu.VMEM((2, zh_n, STATE, ql), BF16),
                pltpu.VMEM((2, zh_n, 1, ql), F32),
                pltpu.VMEM((STATE, ql), BF16),
                pltpu.VMEM((STATE, ql), BF16),
                pltpu.VMEM((2, zl, STATE, ql), BF16),
                pltpu.VMEM((2, zl, STATE, ql), BF16),
                pltpu.VMEM((zl, 2, BLOCK, ql), BF16),
                pltpu.VMEM((8, 128), F32),
                pltpu.VMEM((4, 128, 128), F32),
                pltpu.VMEM((4, 128, 128), F32),
                pltpu.VMEM((4, 128, 128), F32),
                pltpu.VMEM((4, 128, 128), F32),
                pltpu.VMEM((4, 128, 128), F32),
                pltpu.VMEM((4, 128, 128), F32),
                pltpu.VMEM((4, STATE, 128), BF16),
                pltpu.VMEM((4, 128, 128), BF16),
                pltpu.VMEM((4, 8, 128), F32),
                dma((64,)),
                dma((64,)),
                dma((4,)),
                dma((4,)),
                dma((2, 4, 4)),
                dma((2, 4, 4)),
                dma((2, 3, 2)),
                dma((2, 3, 2)),
                dma((13,)),
                dma((4,)),
                dma((4,)),
                dma((4,)),
            ],
            compiler_params=pltpu.CompilerParams(
                collective_id=0, has_side_effects=True, vmem_limit_bytes=67043328
            ),
        )(hidden, in_weight.T, marks, cw, cb, dtb, dec, skip, gain)

    group = P(("fsdp", "batch"), "seq", None)
    rows = P(("fsdp", "batch"), None)
    return jax.shard_map(
        on_device,
        mesh=mesh,
        in_specs=(group, rows, rows, P(), P(), P(), P(), P(), P()),
        out_specs=group,
        check_vma=False,
    )
```

```python
import functools

import jax
import jax.numpy as jnp
from jax import lax
from jax.experimental import pallas as pl
from jax.experimental.pallas import tpu as pltpu
from jax.sharding import PartitionSpec as P

MESH = pl.DeviceIdType.MESH
HEADS = 32
HEAD_DIM = 64
STATE = 64
BLOCK = 128
INNER = 2048
HALF = 1024
PART = 384
HALO = 16
ROWS = 2 * BLOCK + 2 * HALO
F32 = jnp.float32
BF16 = jnp.bfloat16


def kernel(
    cfg,
    hid_ref,
    w_ref,
    marks_in,
    cw_in,
    cb_in,
    dtb_in,
    dec_in,
    skip_in,
    gain_in,
    out_ref,
    marks_ref,
    cw_ref,
    cb_ref,
    dtb_ref,
    dec_ref,
    skip_ref,
    gain_ref,
    wb,
    hidb,
    proj,
    tile,
    other,
    xs,
    ys,
    lk,
    ls,
    fs,
    fb,
    r1,
    rf1,
    gb,
    gf,
    tb,
    tr,
    o4,
    sin,
    outb,
    par,
    cum_s,
    cumt_s,
    stept_s,
    tail_s,
    lead_s,
    msc_s,
    bt_s,
    cr_s,
    fade_s,
    w_ss,
    w_rs,
    h_ss,
    h_rs,
    l_ss,
    l_rs,
    g_ss,
    g_rs,
    in_sem,
    o_ss,
    o_rs,
    own_sem,
):
    nx, ny, nz, zl, zh_n, seqs = cfg
    ql = HALF // zl
    tq = ql // 128
    s = lax.axis_index("seq")
    x = lax.axis_index("fsdp")
    y = lax.axis_index("batch")
    core = lax.rem(s, 2)
    chip = lax.div(s, 2)
    chips = seqs // 2
    z = lax.rem(chip, nz)
    yh = lax.div(chip, nz)
    q = lax.rem(z, zl)
    zh = lax.div(z, zl)

    def dev(seq, xx=x, yy=y):
        return {"seq": seq, "fsdp": xx, "batch": yy}

    def at_z(zz):
        return dev((yh * nz + zz) * 2 + core)

    partner = dev(chip * 2 + 1 - core)
    xp, xm = dev(s, lax.rem(x + 1, nx)), dev(s, lax.rem(x + nx - 1, nx))
    wrap_p = lax.div(y + 1, ny)
    wrap_m = 1 - lax.div(y + ny - 1, ny)
    yp = dev(lax.rem(s + (seqs // 2) * wrap_p, seqs), x, lax.rem(y + 1, ny))
    ym = dev(lax.rem(s + (seqs // 2) * wrap_m, seqs), x, lax.rem(y + ny - 1, ny))
    nxt = lax.rem(chip + 1, chips)
    prv = lax.rem(chip + chips - 1, chips)
    rot = lax.rem(z, 3) if nx > 1 else jnp.int32(0)
    zp, zm = at_z(lax.rem(z + 1, nz)), at_z(lax.rem(z + nz - 1, nz))
    zl_peers = [at_z(zh * zl + lax.rem(q + k, zl)) for k in range(1, zl)]
    zh_peers = [at_z(lax.rem(zh + k, zh_n) * zl + q) for k in range(1, zh_n)]
    y_peer = dev(((1 - yh) * nz + z) * 2 + core)

    barrier = pltpu.get_barrier_semaphore()
    greet = [partner, dev(nxt * 2), dev(nxt * 2 + 1), dev(prv * 2), dev(prv * 2 + 1)]
    greet += zl_peers + zh_peers + [y_peer]
    if nx > 1:
        greet += [xp, xm, yp, ym, zp, zm]
    for peer in greet:
        pl.semaphore_signal(barrier, inc=1, device_id=peer, device_id_type=MESH)

    own_rows = pl.ds(pl.multiple_of(HALO + core * BLOCK, HALO), BLOCK)
    kb = w_ref.shape[1]
    reads = [(hid_ref.at[0], hidb.at[own_rows, :])]
    part_lanes = [
        pl.ds(pl.multiple_of(lax.rem(rot + u, 3) * PART, PART), PART) for u in (1, 2, 0)
    ]
    bases = [lax.rem(p + 5 - rot, 3) * PART for p in range(3)]
    cols0 = core * HALF
    for src, dst, count in (
        (cols0, bases[0], PART),
        (cols0 + PART, bases[1], PART),
        (cols0 + 2 * PART, bases[2], 256),
        (INNER + 128 * core, bases[2] + 256, 32),
        (INNER + 32, bases[2] + 288, 96),
    ):
        reads.append(
            (
                w_ref.at[pl.ds(pl.multiple_of(src, 32), count), :],
                wb.at[0, 0, pl.ds(pl.multiple_of(dst, 32), count), :],
            )
        )
    early = len(reads)
    reads += [
        (marks_in, marks_ref),
        (cw_in, cw_ref),
        (cb_in, cb_ref),
        (dtb_in, dtb_ref),
        (dec_in, dec_ref),
        (skip_in, skip_ref),
        (gain_in, gain_ref),
    ]
    reads = [pltpu.make_async_copy(a, b, in_sem.at[k]) for k, (a, b) in enumerate(reads)]
    for c in reads:
        c.start()
    par[...] = jnp.zeros_like(par)
    fade_s[...] = jnp.zeros_like(fade_s)
    for c in reads[1:early]:
        c.wait()
    pl.semaphore_wait(barrier, len(greet))

    def remote(src, dst, ssem, rsem, peer):
        return pltpu.make_async_remote_copy(
            src_ref=src,
            dst_ref=dst,
            send_sem=ssem,
            recv_sem=rsem,
            device_id=peer,
            device_id_type=MESH,
        )

    sent = []

    msgs = {}
    zmsgs = {}

    def w_send(half, a, b, r0, n, axis, step, tag):
        swap = half == 1
        dim_x = (axis == 1) != swap
        i, j = (b, a) if swap else (a, b)
        ii = (i + step) % nx if dim_x else i
        jj = j if dim_x else (j + step) % ny
        peer = (xp if step > 0 else xm) if dim_x else (yp if step > 0 else ym)
        k = len(msgs)
        rows = pl.ds(half * PART + r0, n)
        copy = remote(
            wb.at[i, j, rows, :], wb.at[ii, jj, rows, :], w_ss.at[k], w_rs.at[k], peer
        )
        copy.start()
        sent.append(copy)
        aa, bb = (jj, ii) if swap else (ii, jj)
        msgs[(half, aa, bb, tag)] = copy

    def w_wait(half, a, b):
        for tag in range(2):
            if (half, a, b, tag) in msgs:
                msgs[(half, a, b, tag)].wait_recv()
        i, j = (b, a) if half == 1 else (a, b)
        k = 32 + len(zmsgs)
        copy = remote(
            wb.at[i, j, pl.ds(half * (PART + hk // 2), hk // 2), :],
            wb.at[i, j, pl.ds(2 * PART + half * (hk // 2), hk // 2), :],
            w_ss.at[k],
            w_rs.at[k],
            zm if half else zp,
        )
        copy.start()
        sent.append(copy)
        zmsgs[(half, i, j)] = copy

    hk = PART
    halves = (0, 1)
    if nx > 1:
        for h in halves:
            w_send(h, 0, 0, 0, hk, 1, 1, 0)
            w_send(h, 0, 0, 0, hk, 1, -1, 0)

    pc = remote(hid_ref.at[0], hidb.at[own_rows, :], h_ss.at[0], h_rs.at[0], partner)
    pc.start()
    sent.append(pc)
    target = core * nxt + (1 - core) * prv
    src_rows = pl.ds(pl.multiple_of((BLOCK - HALO) * core, HALO), HALO)
    dst_rows = pl.ds(pl.multiple_of((HALO + 2 * BLOCK) * (1 - core), HALO), HALO)
    for c in range(2):
        copy = remote(
            hid_ref.at[0, src_rows, :],
            hidb.at[dst_rows, :],
            h_ss.at[1 + c],
            h_rs.at[2 - core],
            dev(target * 2 + c),
        )
        copy.start()
        sent.append(copy)

    def rows_wait():
        reads[0].wait()
        for c in reads[early:]:
            c.wait()
        par[0:2, 0:HEADS] = dtb_ref[...]
        par[2:4, 0:HEADS] = dec_ref[...]
        pc.wait_recv()
        for side in range(2):
            rows = pl.ds((HALO + 2 * BLOCK) * side, HALO)
            remote(
                hid_ref.at[0, 0:HALO, :], hidb.at[rows, :], h_ss.at[1], h_rs.at[1 + side], partner
            ).wait_recv()

    def project(slots, parts, first=False):
        left = []
        for i, j in slots:
            k = lax.rem(x + nx - i, nx) * ny + lax.rem(y + ny - j, ny)
            left.append(hidb[:, pl.ds(pl.multiple_of(k * kb, kb), kb)])
        left = jnp.concatenate(left, axis=1)
        for u in parts:
            rows = slice(u * PART, (u + 1) * PART)
            right = jnp.concatenate([wb[i, j, rows, :] for i, j in slots], axis=1)
            value = lax.dot_general(
                left, right, (((1,), (1,)), ((), ())), preferred_element_type=F32
            )
            if first:
                proj[:, part_lanes[u]] = value
            else:
                proj[:, part_lanes[u]] += value

    if nx > 1:
        xy, zz = (0, 1), (2,)
        order_k = (
            ((0, 0), (0, 1)),
            ((1, 0), (0, 3)),
            ((3, 0), (1, 1)),
            ((3, 3), (1, 3)),
            ((3, 1), (0, 2)),
            ((2, 0), (2, 1)),
            ((1, 2), (3, 2)),
            ((2, 3), (2, 2)),
        )
        for h in halves:
            w_send(h, 0, 0, 0, hk, 2, 1, 0)
            w_send(h, 0, 0, 0, hk, 2, -1, 0)
        for h in halves:
            w_wait(h, 1, 0)
            w_send(h, 1, 0, 0, hk // 2, 1, 1, 0)
            w_wait(h, 3, 0)
            w_send(h, 3, 0, hk // 2, hk // 2, 1, -1, 1)
        for h in halves:
            for a in (1, 3):
                w_send(h, a, 0, 0, hk, 2, 1, 0)
                w_send(h, a, 0, 0, hk, 2, -1, 0)
        rows_wait()
        for h in halves:
            w_wait(h, 0, 1)
            w_send(h, 0, 1, 0, hk, 2, 1, 0)
            w_wait(h, 0, 3)
        project(order_k[0], xy, True)
        for h in halves:
            w_wait(h, 2, 0)
            w_send(h, 2, 0, 0, hk, 2, 1, 0)
            w_send(h, 2, 0, 0, hk, 2, -1, 0)
        project(order_k[1], xy)
        for h in halves:
            w_wait(h, 1, 1)
            w_send(h, 1, 1, 0, hk, 2, 1, 0)
            w_wait(h, 3, 3)
            w_send(h, 3, 3, 0, hk, 2, -1, 0)
        project(order_k[2], xy)
        for h in halves:
            w_wait(h, 1, 3)
            w_wait(h, 3, 1)
        project(order_k[3], xy)
        for h in halves:
            w_wait(h, 2, 3)
            w_send(h, 2, 3, 0, hk, 2, -1, 0)
            w_wait(h, 0, 2)
        project(order_k[4], xy)
        for h in halves:
            w_wait(h, 2, 1)
            w_wait(h, 1, 2)
        project(order_k[5], xy)

        def z_wait(slots):
            for i, j in slots:
                for h in halves:
                    if (i, j) != (0, 0):
                        zmsgs[(h, i, j)].wait_recv()

        z_wait(order_k[0])
        project(order_k[0], zz, True)
        z_wait(order_k[1])
        project(order_k[1], zz)
        for h in halves:
            w_wait(h, 3, 2)
        project(order_k[6], xy)
        for h in halves:
            w_wait(h, 2, 2)
        project(order_k[7], xy)
        for slots in order_k[2:]:
            z_wait(slots)
            project(slots, zz)
    else:
        rows_wait()
        project(((0, 0),), (0, 1, 2), True)

    tile[...] = proj[:, HALF : HALF + 128].astype(BF16)
    swap_tile = remote(tile, other, h_ss.at[3], h_rs.at[3], partner)
    swap_tile.start()
    sent.append(swap_tile)
    first_f = jnp.where(chip == 0, 0.0, 1.0)
    last_f = jnp.where(chip == chips - 1, 0.0, 1.0)

    def ends_off(lanes):
        proj[0:HALO, lanes] = proj[0:HALO, lanes] * first_f
        proj[HALO + 2 * BLOCK :, lanes] = proj[HALO + 2 * BLOCK :, lanes] * last_f

    proj[:, 0:HALF] = proj[:, 0:HALF].astype(BF16).astype(F32)
    ends_off(slice(0, HALF))

    def conv(d, lanes, wlanes):
        total = jnp.broadcast_to(cb_ref[d : d + 1, wlanes], (2 * BLOCK, 128))
        for k in range(4):
            r0 = HALO - 3 + k if d == 0 else HALO + 3 - k
            total = total + cw_ref[d, k : k + 1, wlanes] * proj[pl.ds(r0, 2 * BLOCK), lanes]
        half = 0.5 * total
        return half + half * jnp.tanh(half)

    row_i = lax.broadcasted_iota(jnp.int32, (128, 128), 0)
    lane_i = lax.broadcasted_iota(jnp.int32, (128, 128), 1)
    low = lane_i < HEAD_DIM
    low8 = lax.broadcasted_iota(jnp.int32, (8, 128), 1) < HEAD_DIM
    low1 = lax.broadcasted_iota(jnp.int32, (1, 128), 1) < HEAD_DIM

    def seg_at(v):
        total = jnp.int32(0)
        for m in range(4):
            total = total + jnp.where(marks_ref[0, m] <= v, 1, 0)
        return total

    def pair(value, mask):
        return jnp.where(mask, value[:, 0:1], value[:, 1:2])

    def lanes_of(p):
        return pl.ds(pl.multiple_of(p * 128, 128), 128)

    @pl.loop(0, HALF // 128)
    def _(p):
        wl = pl.ds(pl.multiple_of(core * HALF + p * 128, 128), 128)
        for d in range(2):
            xs[d, :, lanes_of(p)] = conv(d, lanes_of(p), wl).astype(BF16)

    def summary(d, quarter):
        fades_d = [fade_s[d * 2 + d], fade_s[d + 1]]
        for t in range(tq):
            p = quarter * tq + t
            lanes = lanes_of(p)
            inner = slice(t * 128, (t + 1) * 128)
            shift = 128 - 2 * p
            ends, fades = [], []
            for o, j in enumerate((d, 1 - d)):
                n = d * 2 + j
                rows = pl.ds(pl.multiple_of(j * BLOCK, BLOCK), BLOCK)
                tails = pair(pltpu.roll(tail_s[n], shift, 1), low)
                inp = (tails * xs[d, rows, lanes].astype(F32)).astype(BF16)
                ends.append(jnp.dot(bt_s[n], inp, preferred_element_type=F32))
                fades.append(pair(pltpu.roll(fades_d[o], shift, 1), low8)[0:1, :])
            lk[d, :, lanes] = ends[0]
            fb[d, 0:1, lanes] = fades[0]
            ls[d, quarter, :, inner] = (fades[1] * ends[0] + ends[1]).astype(BF16)
            fs[d, quarter, :, inner] = fades[0] * fades[1]

    def half_rows(ch):
        return pl.ds(ch * (STATE // 2), STATE // 2)

    def level1(ph, d):
        copies = [[], []]
        for k in sorted(range(zl), key=lambda k: (k == 0, abs(k - zl // 2))):
            to = lax.rem(q + k, zl)
            summary(d, to)
            if k == 0:
                r1[d, q] = ls[d, q]
                rf1[d, q] = fs[d, q]
                continue
            for ch, src, dst in (
                (0, fs.at[d, to], rf1.at[d, q]),
                (0, ls.at[d, to, half_rows(0)], r1.at[d, q, half_rows(0)]),
                (1, ls.at[d, to, half_rows(1)], r1.at[d, q, half_rows(1)]),
            ):
                a = len(copies[ch]) % 2 if ch == 0 else 0
                c = remote(
                    src, dst, l_ss.at[ph, ch, k, a], l_rs.at[ph, ch, k, a], zl_peers[k - 1]
                )
                c.start()
                sent.append(c)
                copies[ch].append(c)
        return copies

    d_a, d_b = yh, 1 - yh
    swap_tile.wait_recv()
    mine, theirs = tile[...].astype(F32), other[...].astype(F32)
    proj[:, HALF : HALF + 128] = jnp.where(core == 0, mine, theirs)
    proj[:, HALF + 128 :] = jnp.where(core == 0, theirs, mine)
    ends_off(slice(HALF, HALF + 128))

    for d in range(2):
        bc = conv(d, slice(HALF, HALF + 128), slice(INNER, INNER + 128))
        pd = par[d : d + 1, :]
        pr = par[2 + d : 3 + d, :]
        pd = jnp.where(core == 0, pd, pltpu.roll(pd, 112, 1))
        pr = jnp.where(core == 0, pr, pltpu.roll(pr, 112, 1))
        tri = (lane_i <= row_i) if d == 0 else (lane_i >= row_i)
        trif = jnp.where(tri, 1.0, 0.0)
        for j in range(2):
            n = d * 2 + j
            t0 = chip * (2 * BLOCK) + j * BLOCK
            st = proj[HALO + j * BLOCK : HALO + (j + 1) * BLOCK, HALF + 128 :]
            st = jnp.where(core == 0, st, pltpu.roll(st, 112, 1))
            pre = st + pd
            step = jnp.maximum(pre, 0.0) + jnp.log1p(jnp.exp(-jnp.abs(pre)))
            rate = -step * pr
            cum = jnp.dot(
                trif, rate, preferred_element_type=F32, precision=lax.Precision.HIGHEST
            )
            cum_s[n] = cum
            cumt_s[n] = cum.T
            stept_s[n] = step.T
            seg_r = jnp.zeros((128, 128), jnp.int32)
            seg_c = jnp.zeros((128, 128), jnp.int32)
            for m in range(4):
                mark = marks_ref[0, m] - t0
                seg_r = seg_r + jnp.where(row_i >= mark, 1, 0)
                seg_c = seg_c + jnp.where(lane_i >= mark, 1, 0)
            in_seg, out_seg = (
                (seg_at(t0 - 1), seg_at(t0 + BLOCK - 1))
                if d == 0
                else (seg_at(t0 + BLOCK), seg_at(t0))
            )
            last = cum[BLOCK - 1 : BLOCK, :] if d == 0 else cum[0:1, :]
            lead_s[n] = jnp.where(seg_r == in_seg, jnp.exp(cum), 0.0)
            tail_s[n] = jnp.where(seg_r == out_seg, jnp.exp(last - cum), 0.0) * step
            same = jnp.where(in_seg == out_seg, 1.0, 0.0)
            fade_s[n, 0:1, :] = jnp.exp(last) * same
            bcj = bc[j * BLOCK : (j + 1) * BLOCK, :]
            b_only = jnp.where(low, bcj, 0.0).astype(BF16)
            c_low = pltpu.roll(bcj, HEAD_DIM, 1).astype(BF16)
            scores = lax.dot_general(
                c_low, b_only, (((1,), (1,)), ((), ())), preferred_element_type=F32
            )
            msc_s[n] = jnp.where(tri & (seg_r == seg_c), scores, 0.0)
            bt_s[n] = bcj.T[0:STATE, :].astype(BF16)
            cr_s[n] = c_low

    in1a = level1(0, d_a)
    in1b = level1(1, d_b)

    def local_pairs(lo, hi):
        @pl.loop(lo, hi)
        def _(p):
            lanes = lanes_of(p)
            shift = 128 - 2 * p
            head = core * (HEADS // 2) + 2 * p
            for d in range(2):
                skips = jnp.where(low1, skip_ref[d, head], skip_ref[d, head + 1])
                for j in range(2):
                    n = d * 2 + j
                    rows = slice(j * BLOCK, (j + 1) * BLOCK)
                    xt = xs[d, rows, lanes]
                    cums = pltpu.roll(cum_s[n], shift, 1)
                    ws = []
                    for hh in range(2):
                        h = pl.ds(2 * p + hh, 1)
                        gap = jnp.minimum(cums[:, hh : hh + 1] - cumt_s[n, h, :], 0.0)
                        ws.append((jnp.exp(gap) * msc_s[n] * stept_s[n, h, :]).astype(BF16))
                    xf = xt.astype(F32)
                    xl = jnp.where(low, xf, 0.0).astype(BF16)
                    xh = jnp.where(low, 0.0, xf).astype(BF16)
                    inner = jnp.dot(
                        jnp.concatenate(ws, axis=1),
                        jnp.concatenate([xl, xh], axis=0),
                        preferred_element_type=F32,
                    )
                    ys[d, rows, lanes] = inner + skips * xf

    def member(d, step, count):
        return d * (count - 1) + (1 - 2 * d) * step

    def level2(ph, d, copies, ch):
        for c in copies[ch]:
            c.wait_recv()
        total = jnp.zeros((STATE // 2, ql), F32)
        fade = jnp.ones((1, ql), F32)
        for step in range(zl):
            c = member(d, step, zl)
            f = rf1[d, c]
            total = f * total + r1[d, c, half_rows(ch)].astype(F32)
            fade = fade * f
        gb[d, zh, half_rows(ch)] = total.astype(BF16)
        bufs = [gb.at[d, zh, half_rows(ch)]]
        if ch == 0:
            gf[d, zh] = fade
            bufs.append(gf.at[d, zh])
        out = []
        for k in range(1, zh_n):
            for a, buf in enumerate(bufs):
                c = remote(
                    buf, buf, g_ss.at[ph, ch, k, a], g_rs.at[ph, ch, k, a], zh_peers[k - 1]
                )
                c.start()
                sent.append(c)
                out.append(c)
        return out

    def level4(ph, d, state, ch):
        for step in range(zh_n - 1):
            c = member(d, step, zh_n)
            before = (1 - 2 * d) * (zh - c) > 0
            longer = gf[d, c] * state + gb[d, c, half_rows(ch)].astype(F32)
            state = jnp.where(before, longer, state)
        for step in range(zl):
            c = member(d, step, zl)
            o4[d, c, half_rows(ch)] = state.astype(BF16)
            if step < zl - 1:
                state = rf1[d, c] * state + r1[d, c, half_rows(ch)].astype(F32)
        out = []
        for k in range(1, zl):
            to = lax.rem(q + k, zl)
            c = remote(
                o4.at[d, to, half_rows(ch)],
                sin.at[d, q, half_rows(ch)],
                l_ss.at[ph, ch, 0, k],
                l_rs.at[ph, ch, 0, k],
                zl_peers[k - 1],
            )
            c.start()
            sent.append(c)
            out.append(c)
        sin[d, q, half_rows(ch)] = o4[d, q, half_rows(ch)]
        return out

    local_pairs(0, 7)
    in2a = [level2(0, d_a, in1a, ch) for ch in range(2)]
    in2b = [level2(1, d_b, in1b, ch) for ch in range(2)]
    local_pairs(7, 8)
    in3, in4a, in4b = [], [], []
    for ch in range(2):
        for c in in2a[ch]:
            c.wait_recv()
        total = jnp.zeros((STATE // 2, ql), F32)
        for step in range(zh_n):
            c = member(d_a, step, zh_n)
            total = gf[d_a, c] * total + gb[d_a, c, half_rows(ch)].astype(F32)
        tb[half_rows(ch), :] = total.astype(BF16)
        c = remote(
            tb.at[half_rows(ch), :],
            tr.at[half_rows(ch), :],
            g_ss.at[0, ch, 0, 0],
            g_rs.at[0, ch, 0, 0],
            y_peer,
        )
        c.start()
        sent.append(c)
        in3.append(c)
        in4a.append(level4(0, d_a, jnp.zeros((STATE // 2, ql), F32), ch))
    for ch in range(2):
        for c in in2b[ch]:
            c.wait_recv()
        in3[ch].wait_recv()
        in4b.append(level4(1, d_b, tr[half_rows(ch), :].astype(F32), ch))

    row_q = lax.div(lax.broadcasted_iota(jnp.int32, (ql, ql), 0), HEAD_DIM)
    lane_q = lax.div(lax.broadcasted_iota(jnp.int32, (ql, ql), 1), HEAD_DIM)
    ones = jnp.where(row_q == lane_q, 1.0 / HEAD_DIM, 0.0).astype(BF16)

    def finish(quarter, d, last):
        lanes = pl.ds(pl.multiple_of(quarter * ql, ql), ql)
        wl = pl.ds(pl.multiple_of(core * HALF + quarter * ql, ql), ql)
        gains = jnp.where(d == 0, gain_ref[0:1, wl], gain_ref[1:2, wl])
        entering = sin[d, quarter]
        second = fb[d, 0:1, lanes] * entering.astype(F32) + lk[d, :, lanes]
        for j, state in ((d, entering), (1 - d, second.astype(BF16))):
            n = d * 2 + j
            rows = pl.ds(pl.multiple_of(j * BLOCK, BLOCK), BLOCK)
            carried = jnp.dot(cr_s[n, :, 0:STATE], state, preferred_element_type=F32)
            lead = pltpu.roll(lead_s[n], 128 - 2 * tq * quarter, 1)
            leads = jnp.concatenate(
                [
                    jnp.where(low, lead[:, 2 * t : 2 * t + 1], lead[:, 2 * t + 1 : 2 * t + 2])
                    for t in range(tq)
                ],
                axis=1,
            )
            yv = ys[d, rows, lanes] + leads * carried
            mean = jnp.dot((yv * yv).astype(BF16), ones, preferred_element_type=F32)
            res = yv * lax.rsqrt(mean + 1e-05) * gains
            if last:
                outb[quarter, j] = (res + ys[1 - d, rows, lanes]).astype(BF16)
            else:
                ys[d, rows, lanes] = res

    finish(q, d_a, False)
    for k in range(1, zl):
        for ch in range(2):
            in4a[ch][k - 1].wait_recv()
        finish(lax.rem(q + zl - k, zl), d_a, False)
    outs = []
    for k in range(zl):
        quarter = lax.rem(q + zl - k, zl)
        if k > 0:
            for ch in range(2):
                in4b[ch][k - 1].wait_recv()
        finish(quarter, d_b, True)
        cols = pl.ds(pl.multiple_of(core * HALF + quarter * ql, ql), ql)
        oc = remote(
            outb.at[quarter, 1 - core], out_ref.at[0, :, cols], o_ss.at[k], o_rs.at[k], partner
        )
        oc.start()
        own = pltpu.make_async_copy(
            outb.at[quarter, core], out_ref.at[0, :, cols], own_sem.at[k]
        )
        own.start()
        outs.append((oc, own))
    for oc, own in outs:
        own.wait()
        oc.wait()
    for c in sent:
        c.wait_send()


def solution(mesh):
    nx, ny, seqs = mesh.shape["fsdp"], mesh.shape["batch"], mesh.shape["seq"]
    nz = seqs // 4
    zl = 4 if nz % 4 == 0 and nz > 4 else 2
    zh_n = nz // zl
    ql = HALF // zl
    cfg = (nx, ny, nz, zl, zh_n, seqs)

    def on_device(hidden, in_weight, marks, cw, cb, dtb, dec, skip, gain):
        kb = in_weight.shape[0]
        hbm = pl.BlockSpec(memory_space=pl.ANY)
        dma = pltpu.SemaphoreType.DMA
        return pl.pallas_call(
            functools.partial(kernel, cfg),
            out_shape=jax.ShapeDtypeStruct(hidden.shape, BF16),
            in_specs=[hbm] * 9,
            out_specs=hbm,
            scratch_shapes=[
                pltpu.SMEM(marks.shape, jnp.int32),
                pltpu.VMEM(cw.shape, F32),
                pltpu.VMEM(cb.shape, F32),
                pltpu.VMEM(dtb.shape, F32),
                pltpu.VMEM(dec.shape, F32),
                pltpu.SMEM(skip.shape, F32),
                pltpu.VMEM(gain.shape, F32),
                pltpu.VMEM((nx, ny, 3 * PART, kb), BF16),
                pltpu.VMEM((ROWS, INNER), BF16),
                pltpu.VMEM((ROWS, HALF + 256), F32),
                pltpu.VMEM((ROWS, 128), BF16),
                pltpu.VMEM((ROWS, 128), BF16),
                pltpu.VMEM((2, 2 * BLOCK, HALF), BF16),
                pltpu.VMEM((2, 2 * BLOCK, HALF), F32),
                pltpu.VMEM((2, STATE, HALF), F32),
                pltpu.VMEM((2, zl, STATE, ql), BF16),
                pltpu.VMEM((2, zl, 1, ql), F32),
                pltpu.VMEM((2, 8, HALF), F32),
                pltpu.VMEM((2, zl, STATE, ql), BF16),
                pltpu.VMEM((2, zl, 1, ql), F32),
                pltpu.VMEM((2, zh_n, STATE, ql), BF16),
                pltpu.VMEM((2, zh_n, 1, ql), F32),
                pltpu.VMEM((STATE, ql), BF16),
                pltpu.VMEM((STATE, ql), BF16),
                pltpu.VMEM((2, zl, STATE, ql), BF16),
                pltpu.VMEM((2, zl, STATE, ql), BF16),
                pltpu.VMEM((zl, 2, BLOCK, ql), BF16),
                pltpu.VMEM((8, 128), F32),
                pltpu.VMEM((4, 128, 128), F32),
                pltpu.VMEM((4, 128, 128), F32),
                pltpu.VMEM((4, 128, 128), F32),
                pltpu.VMEM((4, 128, 128), F32),
                pltpu.VMEM((4, 128, 128), F32),
                pltpu.VMEM((4, 128, 128), F32),
                pltpu.VMEM((4, STATE, 128), BF16),
                pltpu.VMEM((4, 128, 128), BF16),
                pltpu.VMEM((4, 8, 128), F32),
                dma((64,)),
                dma((64,)),
                dma((4,)),
                dma((4,)),
                dma((2, 2, 4, 4)),
                dma((2, 2, 4, 4)),
                dma((2, 2, 3, 2)),
                dma((2, 2, 3, 2)),
                dma((13,)),
                dma((4,)),
                dma((4,)),
                dma((4,)),
            ],
            compiler_params=pltpu.CompilerParams(
                collective_id=0, has_side_effects=True, vmem_limit_bytes=67043328
            ),
        )(hidden, in_weight.T, marks, cw, cb, dtb, dec, skip, gain)

    group = P(("fsdp", "batch"), "seq", None)
    rows = P(("fsdp", "batch"), None)
    return jax.shard_map(
        on_device,
        mesh=mesh,
        in_specs=(group, rows, rows, P(), P(), P(), P(), P(), P()),
        out_specs=group,
        check_vma=False,
    )
```

```python
import functools

import jax
import jax.numpy as jnp
from jax import lax
from jax.experimental import pallas as pl
from jax.experimental.pallas import tpu as pltpu
from jax.sharding import PartitionSpec as P

MESH = pl.DeviceIdType.MESH
HEADS = 32
HEAD_DIM = 64
STATE = 64
BLOCK = 128
INNER = 2048
HALF = 1024
PART = 384
HALO = 16
ROWS = 2 * BLOCK + 2 * HALO
F32 = jnp.float32
BF16 = jnp.bfloat16


def kernel(
    cfg,
    hid_ref,
    w_ref,
    marks_in,
    cw_in,
    cb_in,
    dtb_in,
    dec_in,
    skip_in,
    gain_in,
    out_ref,
    marks_ref,
    cw_ref,
    cb_ref,
    dtb_ref,
    dec_ref,
    skip_ref,
    gain_ref,
    wb,
    hidb,
    proj,
    tile,
    other,
    xs,
    ys,
    lk,
    ls,
    fs,
    fb,
    r1,
    rf1,
    gb,
    gf,
    tb,
    tr,
    o4,
    sin,
    outb,
    par,
    cum_s,
    cumt_s,
    stept_s,
    tail_s,
    lead_s,
    msc_s,
    bt_s,
    cr_s,
    fade_s,
    w_ss,
    w_rs,
    h_ss,
    h_rs,
    l_ss,
    l_rs,
    g_ss,
    g_rs,
    in_sem,
    o_ss,
    o_rs,
    own_sem,
):
    nx, ny, nz, zl, zh_n, seqs = cfg
    ql = HALF // zl
    tq = ql // 128
    s = lax.axis_index("seq")
    x = lax.axis_index("fsdp")
    y = lax.axis_index("batch")
    core = lax.rem(s, 2)
    chip = lax.div(s, 2)
    chips = seqs // 2
    z = lax.rem(chip, nz)
    yh = lax.div(chip, nz)
    q = lax.rem(z, zl)
    zh = lax.div(z, zl)

    def dev(seq, xx=x, yy=y):
        return {"seq": seq, "fsdp": xx, "batch": yy}

    def at_z(zz):
        return dev((yh * nz + zz) * 2 + core)

    partner = dev(chip * 2 + 1 - core)
    xp, xm = dev(s, lax.rem(x + 1, nx)), dev(s, lax.rem(x + nx - 1, nx))
    wrap_p = lax.div(y + 1, ny)
    wrap_m = 1 - lax.div(y + ny - 1, ny)
    yp = dev(lax.rem(s + (seqs // 2) * wrap_p, seqs), x, lax.rem(y + 1, ny))
    ym = dev(lax.rem(s + (seqs // 2) * wrap_m, seqs), x, lax.rem(y + ny - 1, ny))
    nxt = lax.rem(chip + 1, chips)
    prv = lax.rem(chip + chips - 1, chips)
    rot = lax.rem(z, 3) if nx > 1 else jnp.int32(0)
    zp, zm = at_z(lax.rem(z + 1, nz)), at_z(lax.rem(z + nz - 1, nz))
    zl_peers = [at_z(zh * zl + lax.rem(q + k, zl)) for k in range(1, zl)]
    zh_peers = [at_z(lax.rem(zh + k, zh_n) * zl + q) for k in range(1, zh_n)]
    y_peer = dev(((1 - yh) * nz + z) * 2 + core)

    barrier = pltpu.get_barrier_semaphore()
    greet = [partner, dev(nxt * 2), dev(nxt * 2 + 1), dev(prv * 2), dev(prv * 2 + 1)]
    greet += zl_peers + zh_peers + [y_peer]
    if nx > 1:
        greet += [xp, xm, yp, ym, zp, zm]
    for peer in greet:
        pl.semaphore_signal(barrier, inc=1, device_id=peer, device_id_type=MESH)

    own_rows = pl.ds(pl.multiple_of(HALO + core * BLOCK, HALO), BLOCK)
    kb = w_ref.shape[1]
    reads = [(hid_ref.at[0], hidb.at[own_rows, :])]
    part_lanes = [
        pl.ds(pl.multiple_of(lax.rem(rot + u, 3) * PART, PART), PART) for u in (1, 2, 0)
    ]
    bases = [lax.rem(p + 5 - rot, 3) * PART for p in range(3)]
    cols0 = core * HALF
    for src, dst, count in (
        (cols0, bases[0], PART),
        (cols0 + PART, bases[1], PART),
        (cols0 + 2 * PART, bases[2], 256),
        (INNER + 128 * core, bases[2] + 256, 32),
        (INNER + 32, bases[2] + 288, 96),
    ):
        reads.append(
            (
                w_ref.at[pl.ds(pl.multiple_of(src, 32), count), :],
                wb.at[0, 0, pl.ds(pl.multiple_of(dst, 32), count), :],
            )
        )
    early = len(reads)
    reads += [
        (marks_in, marks_ref),
        (cw_in, cw_ref),
        (cb_in, cb_ref),
        (dtb_in, dtb_ref),
        (dec_in, dec_ref),
        (skip_in, skip_ref),
        (gain_in, gain_ref),
    ]
    reads = [pltpu.make_async_copy(a, b, in_sem.at[k]) for k, (a, b) in enumerate(reads)]
    for c in reads:
        c.start()
    par[...] = jnp.zeros_like(par)
    fade_s[...] = jnp.zeros_like(fade_s)
    for c in reads[1:early]:
        c.wait()
    pl.semaphore_wait(barrier, len(greet))

    def remote(src, dst, ssem, rsem, peer):
        return pltpu.make_async_remote_copy(
            src_ref=src,
            dst_ref=dst,
            send_sem=ssem,
            recv_sem=rsem,
            device_id=peer,
            device_id_type=MESH,
        )

    sent = []

    msgs = {}
    zmsgs = {}

    def w_send(half, a, b, r0, n, axis, step, tag):
        swap = half == 1
        dim_x = (axis == 1) != swap
        i, j = (b, a) if swap else (a, b)
        ii = (i + step) % nx if dim_x else i
        jj = j if dim_x else (j + step) % ny
        peer = (xp if step > 0 else xm) if dim_x else (yp if step > 0 else ym)
        k = len(msgs)
        rows = pl.ds(half * PART + r0, n)
        copy = remote(
            wb.at[i, j, rows, :], wb.at[ii, jj, rows, :], w_ss.at[k], w_rs.at[k], peer
        )
        copy.start()
        sent.append(copy)
        aa, bb = (jj, ii) if swap else (ii, jj)
        msgs[(half, aa, bb, tag)] = copy

    def w_wait(half, a, b):
        for tag in range(2):
            if (half, a, b, tag) in msgs:
                msgs[(half, a, b, tag)].wait_recv()
        i, j = (b, a) if half == 1 else (a, b)
        k = 32 + len(zmsgs)
        copy = remote(
            wb.at[i, j, pl.ds(half * (PART + hk // 2), hk // 2), :],
            wb.at[i, j, pl.ds(2 * PART + half * (hk // 2), hk // 2), :],
            w_ss.at[k],
            w_rs.at[k],
            zm if half else zp,
        )
        copy.start()
        sent.append(copy)
        zmsgs[(half, i, j)] = copy

    hk = PART
    halves = (0, 1)
    if nx > 1:
        for h in halves:
            w_send(h, 0, 0, 0, hk, 1, 1, 0)
            w_send(h, 0, 0, 0, hk, 1, -1, 0)

    pc = remote(hid_ref.at[0], hidb.at[own_rows, :], h_ss.at[0], h_rs.at[0], partner)
    pc.start()
    sent.append(pc)
    target = core * nxt + (1 - core) * prv
    src_rows = pl.ds(pl.multiple_of((BLOCK - HALO) * core, HALO), HALO)
    dst_rows = pl.ds(pl.multiple_of((HALO + 2 * BLOCK) * (1 - core), HALO), HALO)
    for c in range(2):
        copy = remote(
            hid_ref.at[0, src_rows, :],
            hidb.at[dst_rows, :],
            h_ss.at[1 + c],
            h_rs.at[2 - core],
            dev(target * 2 + c),
        )
        copy.start()
        sent.append(copy)

    def rows_wait():
        reads[0].wait()
        for c in reads[early:]:
            c.wait()
        par[0:2, 0:HEADS] = dtb_ref[...]
        par[2:4, 0:HEADS] = dec_ref[...]
        pc.wait_recv()
        for side in range(2):
            rows = pl.ds((HALO + 2 * BLOCK) * side, HALO)
            remote(
                hid_ref.at[0, 0:HALO, :], hidb.at[rows, :], h_ss.at[1], h_rs.at[1 + side], partner
            ).wait_recv()

    def conv(d, lanes, wlanes):
        total = jnp.broadcast_to(cb_ref[d : d + 1, wlanes], (2 * BLOCK, 128))
        for k in range(4):
            r0 = HALO - 3 + k if d == 0 else HALO + 3 - k
            total = total + cw_ref[d, k : k + 1, wlanes] * proj[pl.ds(r0, 2 * BLOCK), lanes]
        return total * jax.nn.sigmoid(total)

    def lanes_of(p):
        return pl.ds(pl.multiple_of(p * 128, 128), 128)

    first_f = jnp.where(chip == 0, 0.0, 1.0)
    last_f = jnp.where(chip == chips - 1, 0.0, 1.0)

    def ends_off(lanes):
        proj[0:HALO, lanes] = proj[0:HALO, lanes] * first_f
        proj[HALO + 2 * BLOCK :, lanes] = proj[HALO + 2 * BLOCK :, lanes] * last_f

    def convolve(u):
        lanes = part_lanes[u]
        proj[:, lanes] = proj[:, lanes].astype(BF16).astype(F32)
        ends_off(lanes)

        @pl.loop(0, PART // 128)
        def _(i):
            p = lax.rem(rot + (u + 1) % 3, 3) * (PART // 128) + i

            @pl.when(p < HALF // 128)
            def _():
                wl = pl.ds(pl.multiple_of(core * HALF + p * 128, 128), 128)
                for d in range(2):
                    xs[d, :, lanes_of(p)] = conv(d, lanes_of(p), wl).astype(BF16)

    def project(slots, parts, first=False):
        left = []
        for i, j in slots:
            k = lax.rem(x + nx - i, nx) * ny + lax.rem(y + ny - j, ny)
            left.append(hidb[:, pl.ds(pl.multiple_of(k * kb, kb), kb)])
        left = jnp.concatenate(left, axis=1)
        for u in parts:
            rows = slice(u * PART, (u + 1) * PART)
            right = jnp.concatenate([wb[i, j, rows, :] for i, j in slots], axis=1)
            value = lax.dot_general(
                left, right, (((1,), (1,)), ((), ())), preferred_element_type=F32
            )
            if first:
                proj[:, part_lanes[u]] = value
            else:
                proj[:, part_lanes[u]] += value

    if nx > 1:
        xy, zz = (0, 1), (2,)
        order_k = (
            ((0, 0), (0, 1)),
            ((1, 0), (0, 3)),
            ((3, 0), (1, 1)),
            ((3, 3), (1, 3)),
            ((3, 1), (0, 2)),
            ((2, 0), (2, 1)),
            ((1, 2), (3, 2)),
            ((2, 3), (2, 2)),
        )
        for h in halves:
            w_send(h, 0, 0, 0, hk, 2, 1, 0)
            w_send(h, 0, 0, 0, hk, 2, -1, 0)
        for h in halves:
            w_wait(h, 1, 0)
            w_send(h, 1, 0, 0, hk // 2, 1, 1, 0)
            w_wait(h, 3, 0)
            w_send(h, 3, 0, hk // 2, hk // 2, 1, -1, 1)
        for h in halves:
            for a in (1, 3):
                w_send(h, a, 0, 0, hk, 2, 1, 0)
                w_send(h, a, 0, 0, hk, 2, -1, 0)
        rows_wait()
        for h in halves:
            w_wait(h, 0, 1)
            w_send(h, 0, 1, 0, hk, 2, 1, 0)
            w_wait(h, 0, 3)
        project(order_k[0], xy, True)
        for h in halves:
            w_wait(h, 2, 0)
            w_send(h, 2, 0, 0, hk, 2, 1, 0)
            w_send(h, 2, 0, 0, hk, 2, -1, 0)
        project(order_k[1], xy)
        for h in halves:
            w_wait(h, 1, 1)
            w_send(h, 1, 1, 0, hk, 2, 1, 0)
            w_wait(h, 3, 3)
            w_send(h, 3, 3, 0, hk, 2, -1, 0)
        project(order_k[2], xy)
        for h in halves:
            w_wait(h, 1, 3)
            w_wait(h, 3, 1)
        project(order_k[3], xy)
        for h in halves:
            w_wait(h, 2, 3)
            w_send(h, 2, 3, 0, hk, 2, -1, 0)
            w_wait(h, 0, 2)
        project(order_k[4], xy)
        for h in halves:
            w_wait(h, 2, 1)
            w_wait(h, 1, 2)
        project(order_k[5], xy)

        def z_wait(slots):
            for i, j in slots:
                for h in halves:
                    if (i, j) != (0, 0):
                        zmsgs[(h, i, j)].wait_recv()

        for h in halves:
            w_wait(h, 3, 2)
        project(order_k[6], xy)
        for h in halves:
            w_wait(h, 2, 2)
        project(order_k[7], xy)
        convolve(0)
        convolve(1)
        for slots in order_k:
            z_wait(slots)
            project(slots, zz, slots is order_k[0])
    else:
        rows_wait()
        project(((0, 0),), (0, 1, 2), True)
        convolve(0)
        convolve(1)

    tile[...] = proj[:, HALF : HALF + 128].astype(BF16)
    swap_tile = remote(tile, other, h_ss.at[3], h_rs.at[3], partner)
    swap_tile.start()
    sent.append(swap_tile)
    convolve(2)
    row_i = lax.broadcasted_iota(jnp.int32, (128, 128), 0)
    lane_i = lax.broadcasted_iota(jnp.int32, (128, 128), 1)
    low = lane_i < HEAD_DIM
    low8 = lax.broadcasted_iota(jnp.int32, (8, 128), 1) < HEAD_DIM
    low1 = lax.broadcasted_iota(jnp.int32, (1, 128), 1) < HEAD_DIM

    def seg_at(v):
        total = jnp.int32(0)
        for m in range(4):
            total = total + jnp.where(marks_ref[0, m] <= v, 1, 0)
        return total

    def pair(value, mask):
        return jnp.where(mask, value[:, 0:1], value[:, 1:2])

    def summary(d, quarter):
        fades_d = [fade_s[d * 2 + d], fade_s[d + 1]]
        for t in range(tq):
            p = quarter * tq + t
            lanes = lanes_of(p)
            inner = slice(t * 128, (t + 1) * 128)
            shift = 128 - 2 * p
            ends, fades = [], []
            for o, j in enumerate((d, 1 - d)):
                n = d * 2 + j
                rows = pl.ds(pl.multiple_of(j * BLOCK, BLOCK), BLOCK)
                tails = pair(pltpu.roll(tail_s[n], shift, 1), low)
                inp = (tails * xs[d, rows, lanes].astype(F32)).astype(BF16)
                ends.append(jnp.dot(bt_s[n], inp, preferred_element_type=F32))
                fades.append(pair(pltpu.roll(fades_d[o], shift, 1), low8)[0:1, :])
            lk[d, :, lanes] = ends[0]
            fb[d, 0:1, lanes] = fades[0]
            ls[d, quarter, :, inner] = (fades[1] * ends[0] + ends[1]).astype(BF16)
            fs[d, quarter, :, inner] = fades[0] * fades[1]

    def level1(ph, d):
        copies = []
        for k in sorted(range(zl), key=lambda k: (k == 0, abs(k - zl // 2))):
            to = lax.rem(q + k, zl)
            summary(d, to)
            if k == 0:
                r1[d, q] = ls[d, q]
                rf1[d, q] = fs[d, q]
                continue
            for a, (src, dst) in enumerate(((ls, r1), (fs, rf1))):
                c = remote(
                    src.at[d, to],
                    dst.at[d, q],
                    l_ss.at[ph, k, a],
                    l_rs.at[ph, k, a],
                    zl_peers[k - 1],
                )
                c.start()
                sent.append(c)
                copies.append(c)
        return copies

    d_a, d_b = yh, 1 - yh
    swap_tile.wait_recv()
    mine, theirs = tile[...].astype(F32), other[...].astype(F32)
    proj[:, HALF : HALF + 128] = jnp.where(core == 0, mine, theirs)
    proj[:, HALF + 128 :] = jnp.where(core == 0, theirs, mine)
    ends_off(slice(HALF, HALF + 128))

    for d in range(2):
        bc = conv(d, slice(HALF, HALF + 128), slice(INNER, INNER + 128))
        pd = par[d : d + 1, :]
        pr = par[2 + d : 3 + d, :]
        pd = jnp.where(core == 0, pd, pltpu.roll(pd, 112, 1))
        pr = jnp.where(core == 0, pr, pltpu.roll(pr, 112, 1))
        tri = (lane_i <= row_i) if d == 0 else (lane_i >= row_i)
        trif = jnp.where(tri, 1.0, 0.0)
        for j in range(2):
            n = d * 2 + j
            t0 = chip * (2 * BLOCK) + j * BLOCK
            st = proj[HALO + j * BLOCK : HALO + (j + 1) * BLOCK, HALF + 128 :]
            st = jnp.where(core == 0, st, pltpu.roll(st, 112, 1))
            pre = st + pd
            step = jnp.maximum(pre, 0.0) + jnp.log1p(jnp.exp(-jnp.abs(pre)))
            rate = -step * pr
            cum = jnp.dot(
                trif, rate, preferred_element_type=F32, precision=lax.Precision.HIGHEST
            )
            cum_s[n] = cum
            cumt_s[n] = cum.T
            stept_s[n] = step.T
            seg_r = jnp.zeros((128, 128), jnp.int32)
            seg_c = jnp.zeros((128, 128), jnp.int32)
            for m in range(4):
                mark = marks_ref[0, m] - t0
                seg_r = seg_r + jnp.where(row_i >= mark, 1, 0)
                seg_c = seg_c + jnp.where(lane_i >= mark, 1, 0)
            in_seg, out_seg = (
                (seg_at(t0 - 1), seg_at(t0 + BLOCK - 1))
                if d == 0
                else (seg_at(t0 + BLOCK), seg_at(t0))
            )
            last = cum[BLOCK - 1 : BLOCK, :] if d == 0 else cum[0:1, :]
            lead_s[n] = jnp.where(seg_r == in_seg, jnp.exp(cum), 0.0)
            tail_s[n] = jnp.where(seg_r == out_seg, jnp.exp(last - cum), 0.0) * step
            same = jnp.where(in_seg == out_seg, 1.0, 0.0)
            fade_s[n, 0:1, :] = jnp.exp(last) * same
            bcj = bc[j * BLOCK : (j + 1) * BLOCK, :]
            b_only = jnp.where(low, bcj, 0.0).astype(BF16)
            c_low = pltpu.roll(bcj, HEAD_DIM, 1).astype(BF16)
            scores = lax.dot_general(
                c_low, b_only, (((1,), (1,)), ((), ())), preferred_element_type=F32
            )
            msc_s[n] = jnp.where(tri & (seg_r == seg_c), scores, 0.0)
            bt_s[n] = bcj.T[0:STATE, :].astype(BF16)
            cr_s[n] = c_low

    in1a = level1(0, d_a)
    in1b = level1(1, d_b)

    def local_pairs(lo, hi):
        @pl.loop(lo, hi)
        def _(p):
            lanes = lanes_of(p)
            shift = 128 - 2 * p
            head = core * (HEADS // 2) + 2 * p
            for d in range(2):
                skips = jnp.where(low1, skip_ref[d, head], skip_ref[d, head + 1])
                for j in range(2):
                    n = d * 2 + j
                    rows = slice(j * BLOCK, (j + 1) * BLOCK)
                    xt = xs[d, rows, lanes]
                    cums = pltpu.roll(cum_s[n], shift, 1)
                    ws = []
                    for hh in range(2):
                        h = pl.ds(2 * p + hh, 1)
                        gap = jnp.minimum(cums[:, hh : hh + 1] - cumt_s[n, h, :], 0.0)
                        ws.append((jnp.exp(gap) * msc_s[n] * stept_s[n, h, :]).astype(BF16))
                    xf = xt.astype(F32)
                    xl = jnp.where(low, xf, 0.0).astype(BF16)
                    xh = jnp.where(low, 0.0, xf).astype(BF16)
                    inner = jnp.dot(
                        jnp.concatenate(ws, axis=1),
                        jnp.concatenate([xl, xh], axis=0),
                        preferred_element_type=F32,
                    )
                    ys[d, rows, lanes] = inner + skips * xf

    def member(d, step, count):
        return d * (count - 1) + (1 - 2 * d) * step

    def level2(ph, d, copies):
        for c in copies:
            c.wait_recv()
        total = jnp.zeros((STATE, ql), F32)
        fade = jnp.ones((1, ql), F32)
        for step in range(zl):
            c = member(d, step, zl)
            f = rf1[d, c]
            total = f * total + r1[d, c].astype(F32)
            fade = fade * f
        gb[d, zh] = total.astype(BF16)
        gf[d, zh] = fade
        out = []
        for k in range(1, zh_n):
            for a, buf in enumerate((gb, gf)):
                c = remote(
                    buf.at[d, zh],
                    buf.at[d, zh],
                    g_ss.at[ph, k, a],
                    g_rs.at[ph, k, a],
                    zh_peers[k - 1],
                )
                c.start()
                sent.append(c)
                out.append(c)
        return out

    def level4(ph, d, state):
        for step in range(zh_n - 1):
            c = member(d, step, zh_n)
            before = (1 - 2 * d) * (zh - c) > 0
            longer = gf[d, c] * state + gb[d, c].astype(F32)
            state = jnp.where(before, longer, state)
        for step in range(zl):
            c = member(d, step, zl)
            o4[d, c] = state.astype(BF16)
            if step < zl - 1:
                state = rf1[d, c] * state + r1[d, c].astype(F32)
        out = []
        for k in range(1, zl):
            to = lax.rem(q + k, zl)
            c = remote(
                o4.at[d, to], sin.at[d, q], l_ss.at[ph, 0, k], l_rs.at[ph, 0, k], zl_peers[k - 1]
            )
            c.start()
            sent.append(c)
            out.append(c)
        sin[d, q] = o4[d, q]
        return out

    local_pairs(0, 4)
    in2a = level2(0, d_a, in1a)
    local_pairs(4, 7)
    in2b = level2(1, d_b, in1b)
    local_pairs(7, 8)
    for c in in2a:
        c.wait_recv()
    total = jnp.zeros((STATE, ql), F32)
    for step in range(zh_n):
        c = member(d_a, step, zh_n)
        total = gf[d_a, c] * total + gb[d_a, c].astype(F32)
    tb[...] = total.astype(BF16)
    in3 = remote(tb, tr, g_ss.at[0, 0, 0], g_rs.at[0, 0, 0], y_peer)
    in3.start()
    sent.append(in3)
    in4a = level4(0, d_a, jnp.zeros((STATE, ql), F32))
    for c in in2b:
        c.wait_recv()
    in3.wait_recv()
    in4b = level4(1, d_b, tr[...].astype(F32))

    row_q = lax.div(lax.broadcasted_iota(jnp.int32, (ql, ql), 0), HEAD_DIM)
    lane_q = lax.div(lax.broadcasted_iota(jnp.int32, (ql, ql), 1), HEAD_DIM)
    ones = jnp.where(row_q == lane_q, 1.0 / HEAD_DIM, 0.0).astype(BF16)

    def finish(quarter, d, last):
        lanes = pl.ds(pl.multiple_of(quarter * ql, ql), ql)
        wl = pl.ds(pl.multiple_of(core * HALF + quarter * ql, ql), ql)
        gains = jnp.where(d == 0, gain_ref[0:1, wl], gain_ref[1:2, wl])
        entering = sin[d, quarter]
        second = fb[d, 0:1, lanes] * entering.astype(F32) + lk[d, :, lanes]
        for j, state in ((d, entering), (1 - d, second.astype(BF16))):
            n = d * 2 + j
            rows = pl.ds(pl.multiple_of(j * BLOCK, BLOCK), BLOCK)
            carried = jnp.dot(cr_s[n, :, 0:STATE], state, preferred_element_type=F32)
            lead = pltpu.roll(lead_s[n], 128 - 2 * tq * quarter, 1)
            leads = jnp.concatenate(
                [
                    jnp.where(low, lead[:, 2 * t : 2 * t + 1], lead[:, 2 * t + 1 : 2 * t + 2])
                    for t in range(tq)
                ],
                axis=1,
            )
            yv = ys[d, rows, lanes] + leads * carried
            mean = jnp.dot((yv * yv).astype(BF16), ones, preferred_element_type=F32)
            res = yv * lax.rsqrt(mean + 1e-05) * gains
            if last:
                outb[quarter, j] = (res + ys[1 - d, rows, lanes]).astype(BF16)
            else:
                ys[d, rows, lanes] = res

    finish(q, d_a, False)
    for k in range(1, zl):
        in4a[k - 1].wait_recv()
        finish(lax.rem(q + zl - k, zl), d_a, False)
    outs = []
    for k in range(zl):
        quarter = lax.rem(q + zl - k, zl)
        if k > 0:
            in4b[k - 1].wait_recv()
        finish(quarter, d_b, True)
        cols = pl.ds(pl.multiple_of(core * HALF + quarter * ql, ql), ql)
        oc = remote(
            outb.at[quarter, 1 - core], out_ref.at[0, :, cols], o_ss.at[k], o_rs.at[k], partner
        )
        oc.start()
        own = pltpu.make_async_copy(
            outb.at[quarter, core], out_ref.at[0, :, cols], own_sem.at[k]
        )
        own.start()
        outs.append((oc, own))
    for oc, own in outs:
        own.wait()
        oc.wait()
    for c in sent:
        c.wait_send()


def solution(mesh):
    nx, ny, seqs = mesh.shape["fsdp"], mesh.shape["batch"], mesh.shape["seq"]
    nz = seqs // 4
    zl = 4 if nz % 4 == 0 and nz > 4 else 2
    zh_n = nz // zl
    ql = HALF // zl
    cfg = (nx, ny, nz, zl, zh_n, seqs)

    def on_device(hidden, in_weight, marks, cw, cb, dtb, dec, skip, gain):
        kb = in_weight.shape[0]
        hbm = pl.BlockSpec(memory_space=pl.ANY)
        dma = pltpu.SemaphoreType.DMA
        return pl.pallas_call(
            functools.partial(kernel, cfg),
            out_shape=jax.ShapeDtypeStruct(hidden.shape, BF16),
            in_specs=[hbm] * 9,
            out_specs=hbm,
            scratch_shapes=[
                pltpu.SMEM(marks.shape, jnp.int32),
                pltpu.VMEM(cw.shape, F32),
                pltpu.VMEM(cb.shape, F32),
                pltpu.VMEM(dtb.shape, F32),
                pltpu.VMEM(dec.shape, F32),
                pltpu.SMEM(skip.shape, F32),
                pltpu.VMEM(gain.shape, F32),
                pltpu.VMEM((nx, ny, 3 * PART, kb), BF16),
                pltpu.VMEM((ROWS, INNER), BF16),
                pltpu.VMEM((ROWS, HALF + 256), F32),
                pltpu.VMEM((ROWS, 128), BF16),
                pltpu.VMEM((ROWS, 128), BF16),
                pltpu.VMEM((2, 2 * BLOCK, HALF), BF16),
                pltpu.VMEM((2, 2 * BLOCK, HALF), F32),
                pltpu.VMEM((2, STATE, HALF), F32),
                pltpu.VMEM((2, zl, STATE, ql), BF16),
                pltpu.VMEM((2, zl, 1, ql), F32),
                pltpu.VMEM((2, 8, HALF), F32),
                pltpu.VMEM((2, zl, STATE, ql), BF16),
                pltpu.VMEM((2, zl, 1, ql), F32),
                pltpu.VMEM((2, zh_n, STATE, ql), BF16),
                pltpu.VMEM((2, zh_n, 1, ql), F32),
                pltpu.VMEM((STATE, ql), BF16),
                pltpu.VMEM((STATE, ql), BF16),
                pltpu.VMEM((2, zl, STATE, ql), BF16),
                pltpu.VMEM((2, zl, STATE, ql), BF16),
                pltpu.VMEM((zl, 2, BLOCK, ql), BF16),
                pltpu.VMEM((8, 128), F32),
                pltpu.VMEM((4, 128, 128), F32),
                pltpu.VMEM((4, 128, 128), F32),
                pltpu.VMEM((4, 128, 128), F32),
                pltpu.VMEM((4, 128, 128), F32),
                pltpu.VMEM((4, 128, 128), F32),
                pltpu.VMEM((4, 128, 128), F32),
                pltpu.VMEM((4, STATE, 128), BF16),
                pltpu.VMEM((4, 128, 128), BF16),
                pltpu.VMEM((4, 8, 128), F32),
                dma((64,)),
                dma((64,)),
                dma((4,)),
                dma((4,)),
                dma((2, 4, 4)),
                dma((2, 4, 4)),
                dma((2, 3, 2)),
                dma((2, 3, 2)),
                dma((13,)),
                dma((4,)),
                dma((4,)),
                dma((4,)),
            ],
            compiler_params=pltpu.CompilerParams(
                collective_id=0, has_side_effects=True, vmem_limit_bytes=67043328
            ),
        )(hidden, in_weight.T, marks, cw, cb, dtb, dec, skip, gain)

    group = P(("fsdp", "batch"), "seq", None)
    rows = P(("fsdp", "batch"), None)
    return jax.shard_map(
        on_device,
        mesh=mesh,
        in_specs=(group, rows, rows, P(), P(), P(), P(), P(), P()),
        out_specs=group,
        check_vma=False,
    )
```

```python
import functools

import jax
import jax.numpy as jnp
from jax import lax
from jax.experimental import pallas as pl
from jax.experimental.pallas import tpu as pltpu
from jax.sharding import PartitionSpec as P

MESH = pl.DeviceIdType.MESH
HEADS = 32
HEAD_DIM = 64
STATE = 64
BLOCK = 128
INNER = 2048
HALF = 1024
PART = 384
HALO = 16
ROWS = 2 * BLOCK + 2 * HALO
F32 = jnp.float32
BF16 = jnp.bfloat16


def kernel(
    cfg,
    hid_ref,
    w_ref,
    marks_in,
    cw_in,
    cb_in,
    dtb_in,
    dec_in,
    skip_in,
    gain_in,
    out_ref,
    marks_ref,
    cw_ref,
    cb_ref,
    dtb_ref,
    dec_ref,
    skip_ref,
    gain_ref,
    wb,
    hidb,
    proj,
    tile,
    other,
    xs,
    ys,
    lk,
    ls,
    fs,
    fb,
    r1,
    rf1,
    gb,
    gf,
    tb,
    tr,
    o4,
    sin,
    outb,
    par,
    cum_s,
    cumt_s,
    stept_s,
    tail_s,
    lead_s,
    msc_s,
    bt_s,
    cr_s,
    fade_s,
    w_ss,
    w_rs,
    h_ss,
    h_rs,
    l_ss,
    l_rs,
    g_ss,
    g_rs,
    in_sem,
    o_ss,
    o_rs,
    own_sem,
):
    nx, ny, nz, zl, zh_n, seqs = cfg
    ql = HALF // zl
    tq = ql // 128
    s = lax.axis_index("seq")
    x = lax.axis_index("fsdp")
    y = lax.axis_index("batch")
    core = lax.rem(s, 2)
    chip = lax.div(s, 2)
    chips = seqs // 2
    z = lax.rem(chip, nz)
    yh = lax.div(chip, nz)
    q = lax.rem(z, zl)
    zh = lax.div(z, zl)

    def dev(seq, xx=x, yy=y):
        return {"seq": seq, "fsdp": xx, "batch": yy}

    def at_z(zz):
        return dev((yh * nz + zz) * 2 + core)

    partner = dev(chip * 2 + 1 - core)
    xp, xm = dev(s, lax.rem(x + 1, nx)), dev(s, lax.rem(x + nx - 1, nx))
    wrap_p = lax.div(y + 1, ny)
    wrap_m = 1 - lax.div(y + ny - 1, ny)
    yp = dev(lax.rem(s + (seqs // 2) * wrap_p, seqs), x, lax.rem(y + 1, ny))
    ym = dev(lax.rem(s + (seqs // 2) * wrap_m, seqs), x, lax.rem(y + ny - 1, ny))
    nxt = lax.rem(chip + 1, chips)
    prv = lax.rem(chip + chips - 1, chips)
    rot = lax.rem(z, 3) if nx > 1 else jnp.int32(0)
    zp, zm = at_z(lax.rem(z + 1, nz)), at_z(lax.rem(z + nz - 1, nz))
    zl_peers = [at_z(zh * zl + lax.rem(q + k, zl)) for k in range(1, zl)]
    zh_peers = [at_z(lax.rem(zh + k, zh_n) * zl + q) for k in range(1, zh_n)]
    y_peer = dev(((1 - yh) * nz + z) * 2 + core)

    barrier = pltpu.get_barrier_semaphore()
    greet = [partner, dev(nxt * 2), dev(nxt * 2 + 1), dev(prv * 2), dev(prv * 2 + 1)]
    greet += zl_peers + zh_peers + [y_peer]
    if nx > 1:
        greet += [xp, xm, yp, ym, zp, zm]
    for peer in greet:
        pl.semaphore_signal(barrier, inc=1, device_id=peer, device_id_type=MESH)

    own_rows = pl.ds(pl.multiple_of(HALO + core * BLOCK, HALO), BLOCK)
    kb = w_ref.shape[1]
    reads = [(hid_ref.at[0], hidb.at[own_rows, :])]
    part_lanes = [
        pl.ds(pl.multiple_of(lax.rem(rot + u, 3) * PART, PART), PART) for u in (1, 2, 0)
    ]
    bases = [lax.rem(p + 5 - rot, 3) * PART for p in range(3)]
    cols0 = core * HALF
    for src, dst, count in (
        (cols0, bases[0], PART),
        (cols0 + PART, bases[1], PART),
        (cols0 + 2 * PART, bases[2], 256),
        (INNER + 128 * core, bases[2] + 256, 32),
        (INNER + 32, bases[2] + 288, 96),
    ):
        reads.append(
            (
                w_ref.at[pl.ds(pl.multiple_of(src, 32), count), :],
                wb.at[0, 0, pl.ds(pl.multiple_of(dst, 32), count), :],
            )
        )
    early = len(reads)
    reads += [
        (marks_in, marks_ref),
        (cw_in, cw_ref),
        (cb_in, cb_ref),
        (dtb_in, dtb_ref),
        (dec_in, dec_ref),
        (skip_in, skip_ref),
        (gain_in, gain_ref),
    ]
    reads = [pltpu.make_async_copy(a, b, in_sem.at[k]) for k, (a, b) in enumerate(reads)]
    for c in reads:
        c.start()
    par[...] = jnp.zeros_like(par)
    fade_s[...] = jnp.zeros_like(fade_s)
    for c in reads[1:early]:
        c.wait()
    pl.semaphore_wait(barrier, len(greet))

    def remote(src, dst, ssem, rsem, peer):
        return pltpu.make_async_remote_copy(
            src_ref=src,
            dst_ref=dst,
            send_sem=ssem,
            recv_sem=rsem,
            device_id=peer,
            device_id_type=MESH,
        )

    sent = []

    msgs = {}
    zmsgs = {}

    def w_send(half, a, b, r0, n, axis, step, tag):
        swap = half == 1
        dim_x = (axis == 1) != swap
        i, j = (b, a) if swap else (a, b)
        ii = (i + step) % nx if dim_x else i
        jj = j if dim_x else (j + step) % ny
        peer = (xp if step > 0 else xm) if dim_x else (yp if step > 0 else ym)
        k = len(msgs)
        rows = pl.ds(half * PART + r0, n)
        copy = remote(
            wb.at[i, j, rows, :], wb.at[ii, jj, rows, :], w_ss.at[k], w_rs.at[k], peer
        )
        copy.start()
        sent.append(copy)
        aa, bb = (jj, ii) if swap else (ii, jj)
        msgs[(half, aa, bb, tag)] = copy

    def w_wait(half, a, b):
        for tag in range(2):
            if (half, a, b, tag) in msgs:
                msgs[(half, a, b, tag)].wait_recv()
        i, j = (b, a) if half == 1 else (a, b)
        k = 32 + len(zmsgs)
        copy = remote(
            wb.at[i, j, pl.ds(half * (PART + hk // 2), hk // 2), :],
            wb.at[i, j, pl.ds(2 * PART + half * (hk // 2), hk // 2), :],
            w_ss.at[k],
            w_rs.at[k],
            zm if half else zp,
        )
        copy.start()
        sent.append(copy)
        zmsgs[(half, i, j)] = copy

    hk = PART
    halves = (0, 1)
    if nx > 1:
        for h in halves:
            w_send(h, 0, 0, 0, hk, 1, 1, 0)
            w_send(h, 0, 0, 0, hk, 1, -1, 0)

    pc = remote(hid_ref.at[0], hidb.at[own_rows, :], h_ss.at[0], h_rs.at[0], partner)
    pc.start()
    sent.append(pc)
    target = core * nxt + (1 - core) * prv
    src_rows = pl.ds(pl.multiple_of((BLOCK - HALO) * core, HALO), HALO)
    dst_rows = pl.ds(pl.multiple_of((HALO + 2 * BLOCK) * (1 - core), HALO), HALO)
    for c in range(2):
        copy = remote(
            hid_ref.at[0, src_rows, :],
            hidb.at[dst_rows, :],
            h_ss.at[1 + c],
            h_rs.at[2 - core],
            dev(target * 2 + c),
        )
        copy.start()
        sent.append(copy)

    def rows_wait():
        reads[0].wait()
        for c in reads[early:]:
            c.wait()
        par[0:2, 0:HEADS] = dtb_ref[...]
        par[2:4, 0:HEADS] = dec_ref[...]
        pc.wait_recv()
        for side in range(2):
            rows = pl.ds((HALO + 2 * BLOCK) * side, HALO)
            remote(
                hid_ref.at[0, 0:HALO, :], hidb.at[rows, :], h_ss.at[1], h_rs.at[1 + side], partner
            ).wait_recv()

    def conv(d, lanes, wlanes):
        total = jnp.broadcast_to(cb_ref[d : d + 1, wlanes], (2 * BLOCK, 128))
        for k in range(4):
            r0 = HALO - 3 + k if d == 0 else HALO + 3 - k
            total = total + cw_ref[d, k : k + 1, wlanes] * proj[pl.ds(r0, 2 * BLOCK), lanes]
        return total * jax.nn.sigmoid(total)

    def lanes_of(p):
        return pl.ds(pl.multiple_of(p * 128, 128), 128)

    first_f = jnp.where(chip == 0, 0.0, 1.0)
    last_f = jnp.where(chip == chips - 1, 0.0, 1.0)

    def ends_off(lanes):
        proj[0:HALO, lanes] = proj[0:HALO, lanes] * first_f
        proj[HALO + 2 * BLOCK :, lanes] = proj[HALO + 2 * BLOCK :, lanes] * last_f

    def convolve(u):
        lanes = part_lanes[u]
        proj[:, lanes] = proj[:, lanes].astype(BF16).astype(F32)
        ends_off(lanes)

        @pl.loop(0, PART // 128)
        def _(i):
            p = lax.rem(rot + (u + 1) % 3, 3) * (PART // 128) + i

            @pl.when(p < HALF // 128)
            def _():
                wl = pl.ds(pl.multiple_of(core * HALF + p * 128, 128), 128)
                for d in range(2):
                    xs[d, :, lanes_of(p)] = conv(d, lanes_of(p), wl).astype(BF16)

    def project(slots, parts, first=False):
        left = []
        for i, j in slots:
            k = lax.rem(x + nx - i, nx) * ny + lax.rem(y + ny - j, ny)
            left.append(hidb[:, pl.ds(pl.multiple_of(k * kb, kb), kb)])
        left = jnp.concatenate(left, axis=1)
        for u in parts:
            rows = slice(u * PART, (u + 1) * PART)
            right = jnp.concatenate([wb[i, j, rows, :] for i, j in slots], axis=1)
            value = lax.dot_general(
                left, right, (((1,), (1,)), ((), ())), preferred_element_type=F32
            )
            if first:
                proj[:, part_lanes[u]] = value
            else:
                proj[:, part_lanes[u]] += value

    if nx > 1:
        xy, zz = (0, 1), (2,)
        order_k = (
            ((0, 0), (0, 1)),
            ((1, 0), (0, 3)),
            ((3, 0), (1, 1)),
            ((3, 3), (1, 3)),
            ((3, 1), (0, 2)),
            ((2, 0), (2, 1)),
            ((1, 2), (3, 2)),
            ((2, 3), (2, 2)),
        )
        for h in halves:
            w_send(h, 0, 0, 0, hk, 2, 1, 0)
            w_send(h, 0, 0, 0, hk, 2, -1, 0)
        for h in halves:
            w_wait(h, 1, 0)
            w_send(h, 1, 0, 0, hk // 2, 1, 1, 0)
            w_wait(h, 3, 0)
            w_send(h, 3, 0, hk // 2, hk // 2, 1, -1, 1)
        for h in halves:
            for a in (1, 3):
                w_send(h, a, 0, 0, hk, 2, 1, 0)
                w_send(h, a, 0, 0, hk, 2, -1, 0)
        rows_wait()
        for h in halves:
            w_wait(h, 0, 1)
            w_send(h, 0, 1, 0, hk, 2, 1, 0)
            w_wait(h, 0, 3)
        project(order_k[0], xy, True)
        for h in halves:
            w_wait(h, 2, 0)
            w_send(h, 2, 0, 0, hk, 2, 1, 0)
            w_send(h, 2, 0, 0, hk, 2, -1, 0)
        project(order_k[1], xy)
        for h in halves:
            w_wait(h, 1, 1)
            w_send(h, 1, 1, 0, hk, 2, 1, 0)
            w_wait(h, 3, 3)
            w_send(h, 3, 3, 0, hk, 2, -1, 0)
        project(order_k[2], xy)
        for h in halves:
            w_wait(h, 1, 3)
            w_wait(h, 3, 1)
        project(order_k[3], xy)
        for h in halves:
            w_wait(h, 2, 3)
            w_send(h, 2, 3, 0, hk, 2, -1, 0)
            w_wait(h, 0, 2)
        project(order_k[4], xy)
        for h in halves:
            w_wait(h, 2, 1)
            w_wait(h, 1, 2)
        project(order_k[5], xy)

        def z_wait(slots):
            for i, j in slots:
                for h in halves:
                    if (i, j) != (0, 0):
                        zmsgs[(h, i, j)].wait_recv()

        for h in halves:
            w_wait(h, 3, 2)
        project(order_k[6], xy)
        for h in halves:
            w_wait(h, 2, 2)
        project(order_k[7], xy)
        convolve(0)
        convolve(1)
        for slots in order_k:
            z_wait(slots)
            project(slots, zz, slots is order_k[0])
    else:
        rows_wait()
        project(((0, 0),), (0, 1, 2), True)
        convolve(0)
        convolve(1)

    tile[...] = proj[:, HALF : HALF + 128].astype(BF16)
    swap_tile = remote(tile, other, h_ss.at[3], h_rs.at[3], partner)
    swap_tile.start()
    sent.append(swap_tile)
    convolve(2)
    row_i = lax.broadcasted_iota(jnp.int32, (128, 128), 0)
    lane_i = lax.broadcasted_iota(jnp.int32, (128, 128), 1)
    low = lane_i < HEAD_DIM
    low8 = lax.broadcasted_iota(jnp.int32, (8, 128), 1) < HEAD_DIM
    low1 = lax.broadcasted_iota(jnp.int32, (1, 128), 1) < HEAD_DIM

    def seg_at(v):
        total = jnp.int32(0)
        for m in range(4):
            total = total + jnp.where(marks_ref[0, m] <= v, 1, 0)
        return total

    def pair(value, mask):
        return jnp.where(mask, value[:, 0:1], value[:, 1:2])

    def summary(d, quarter):
        fades_d = [fade_s[d * 2 + d], fade_s[d + 1]]
        for t in range(tq):
            p = quarter * tq + t
            lanes = lanes_of(p)
            inner = slice(t * 128, (t + 1) * 128)
            shift = 128 - 2 * p
            ends, fades = [], []
            for o, j in enumerate((d, 1 - d)):
                n = d * 2 + j
                rows = pl.ds(pl.multiple_of(j * BLOCK, BLOCK), BLOCK)
                tails = pair(pltpu.roll(tail_s[n], shift, 1), low)
                inp = (tails * xs[d, rows, lanes].astype(F32)).astype(BF16)
                ends.append(jnp.dot(bt_s[n], inp, preferred_element_type=F32))
                fades.append(pair(pltpu.roll(fades_d[o], shift, 1), low8)[0:1, :])
            lk[d, :, lanes] = ends[0]
            fb[d, 0:1, lanes] = fades[0]
            ls[d, quarter, :, inner] = (fades[1] * ends[0] + ends[1]).astype(BF16)
            fs[d, quarter, :, inner] = fades[0] * fades[1]

    def level1(ph, d):
        copies = []
        for k in sorted(range(zl), key=lambda k: (k == 0, abs(k - zl // 2))):
            to = lax.rem(q + k, zl)
            summary(d, to)
            if k == 0:
                r1[d, q] = ls[d, q]
                rf1[d, q] = fs[d, q]
                continue
            for a, (src, dst) in enumerate(((ls, r1), (fs, rf1))):
                c = remote(
                    src.at[d, to],
                    dst.at[d, q],
                    l_ss.at[ph, k, a],
                    l_rs.at[ph, k, a],
                    zl_peers[k - 1],
                )
                c.start()
                sent.append(c)
                copies.append(c)
        return copies

    d_a, d_b = yh, 1 - yh
    swap_tile.wait_recv()
    mine, theirs = tile[...].astype(F32), other[...].astype(F32)
    proj[:, HALF : HALF + 128] = jnp.where(core == 0, mine, theirs)
    proj[:, HALF + 128 :] = jnp.where(core == 0, theirs, mine)
    ends_off(slice(HALF, HALF + 128))

    for d in range(2):
        bc = conv(d, slice(HALF, HALF + 128), slice(INNER, INNER + 128))
        pd = par[d : d + 1, :]
        pr = par[2 + d : 3 + d, :]
        pd = jnp.where(core == 0, pd, pltpu.roll(pd, 112, 1))
        pr = jnp.where(core == 0, pr, pltpu.roll(pr, 112, 1))
        tri = (lane_i <= row_i) if d == 0 else (lane_i >= row_i)
        trif = jnp.where(tri, 1.0, 0.0)
        for j in range(2):
            n = d * 2 + j
            t0 = chip * (2 * BLOCK) + j * BLOCK
            st = proj[HALO + j * BLOCK : HALO + (j + 1) * BLOCK, HALF + 128 :]
            st = jnp.where(core == 0, st, pltpu.roll(st, 112, 1))
            pre = st + pd
            step = jnp.maximum(pre, 0.0) + jnp.log1p(jnp.exp(-jnp.abs(pre)))
            rate = -step * pr
            cum = jnp.dot(
                trif, rate, preferred_element_type=F32, precision=lax.Precision.HIGHEST
            )
            cum_s[n] = cum
            cumt_s[n] = cum.T
            stept_s[n] = step.T
            seg_r = jnp.zeros((128, 128), jnp.int32)
            seg_c = jnp.zeros((128, 128), jnp.int32)
            for m in range(4):
                mark = marks_ref[0, m] - t0
                seg_r = seg_r + jnp.where(row_i >= mark, 1, 0)
                seg_c = seg_c + jnp.where(lane_i >= mark, 1, 0)
            in_seg, out_seg = (
                (seg_at(t0 - 1), seg_at(t0 + BLOCK - 1))
                if d == 0
                else (seg_at(t0 + BLOCK), seg_at(t0))
            )
            last = cum[BLOCK - 1 : BLOCK, :] if d == 0 else cum[0:1, :]
            lead_s[n] = jnp.where(seg_r == in_seg, jnp.exp(cum), 0.0)
            tail_s[n] = jnp.where(seg_r == out_seg, jnp.exp(last - cum), 0.0) * step
            same = jnp.where(in_seg == out_seg, 1.0, 0.0)
            fade_s[n, 0:1, :] = jnp.exp(last) * same
            bcj = bc[j * BLOCK : (j + 1) * BLOCK, :]
            b_only = jnp.where(low, bcj, 0.0).astype(BF16)
            c_low = pltpu.roll(bcj, HEAD_DIM, 1).astype(BF16)
            scores = lax.dot_general(
                c_low, b_only, (((1,), (1,)), ((), ())), preferred_element_type=F32
            )
            msc_s[n] = jnp.where(tri & (seg_r == seg_c), scores, 0.0)
            bt_s[n] = bcj.T[0:STATE, :].astype(BF16)
            cr_s[n] = c_low

    in1a = level1(0, d_a)
    in1b = level1(1, d_b)

    def local_pairs(lo, hi):
        @pl.loop(lo, hi)
        def _(p):
            lanes = lanes_of(p)
            shift = 128 - 2 * p
            head = core * (HEADS // 2) + 2 * p
            for d in range(2):
                skips = jnp.where(low1, skip_ref[d, head], skip_ref[d, head + 1])
                for j in range(2):
                    n = d * 2 + j
                    rows = slice(j * BLOCK, (j + 1) * BLOCK)
                    xt = xs[d, rows, lanes]
                    cums = pltpu.roll(cum_s[n], shift, 1)
                    ws = []
                    for hh in range(2):
                        h = pl.ds(2 * p + hh, 1)
                        gap = jnp.minimum(cums[:, hh : hh + 1] - cumt_s[n, h, :], 0.0)
                        ws.append((jnp.exp(gap) * msc_s[n] * stept_s[n, h, :]).astype(BF16))
                    xf = xt.astype(F32)
                    xl = jnp.where(low, xf, 0.0).astype(BF16)
                    xh = jnp.where(low, 0.0, xf).astype(BF16)
                    inner = jnp.dot(
                        jnp.concatenate(ws, axis=1),
                        jnp.concatenate([xl, xh], axis=0),
                        preferred_element_type=F32,
                    )
                    ys[d, rows, lanes] = inner + skips * xf

    def member(d, step, count):
        return d * (count - 1) + (1 - 2 * d) * step

    def level2(ph, d, copies):
        for c in copies:
            c.wait_recv()
        total = jnp.zeros((STATE, ql), F32)
        fade = jnp.ones((1, ql), F32)
        for step in range(zl):
            c = member(d, step, zl)
            f = rf1[d, c]
            total = f * total + r1[d, c].astype(F32)
            fade = fade * f
        gb[d, zh] = total.astype(BF16)
        gf[d, zh] = fade
        out = []
        for k in range(1, zh_n):
            for a, buf in enumerate((gb, gf)):
                c = remote(
                    buf.at[d, zh],
                    buf.at[d, zh],
                    g_ss.at[ph, k, a],
                    g_rs.at[ph, k, a],
                    zh_peers[k - 1],
                )
                c.start()
                sent.append(c)
                out.append(c)
        return out

    def level4(ph, d, state):
        for step in range(zh_n - 1):
            c = member(d, step, zh_n)
            before = (1 - 2 * d) * (zh - c) > 0
            longer = gf[d, c] * state + gb[d, c].astype(F32)
            state = jnp.where(before, longer, state)
        for step in range(zl):
            c = member(d, step, zl)
            o4[d, c] = state.astype(BF16)
            if step < zl - 1:
                state = rf1[d, c] * state + r1[d, c].astype(F32)
        out = []
        for k in range(1, zl):
            to = lax.rem(q + k, zl)
            c = remote(
                o4.at[d, to], sin.at[d, q], l_ss.at[ph, 0, k], l_rs.at[ph, 0, k], zl_peers[k - 1]
            )
            c.start()
            sent.append(c)
            out.append(c)
        sin[d, q] = o4[d, q]
        return out

    local_pairs(0, 5)
    in2a = level2(0, d_a, in1a)
    in2b = level2(1, d_b, in1b)
    local_pairs(5, 8)
    for c in in2a:
        c.wait_recv()
    total = jnp.zeros((STATE, ql), F32)
    for step in range(zh_n):
        c = member(d_a, step, zh_n)
        total = gf[d_a, c] * total + gb[d_a, c].astype(F32)
    tb[...] = total.astype(BF16)
    in3 = remote(tb, tr, g_ss.at[0, 0, 0], g_rs.at[0, 0, 0], y_peer)
    in3.start()
    sent.append(in3)
    in4a = level4(0, d_a, jnp.zeros((STATE, ql), F32))
    for c in in2b:
        c.wait_recv()
    in3.wait_recv()
    in4b = level4(1, d_b, tr[...].astype(F32))

    row_q = lax.div(lax.broadcasted_iota(jnp.int32, (ql, ql), 0), HEAD_DIM)
    lane_q = lax.div(lax.broadcasted_iota(jnp.int32, (ql, ql), 1), HEAD_DIM)
    ones = jnp.where(row_q == lane_q, 1.0 / HEAD_DIM, 0.0).astype(BF16)

    def finish(quarter, d, last):
        lanes = pl.ds(pl.multiple_of(quarter * ql, ql), ql)
        wl = pl.ds(pl.multiple_of(core * HALF + quarter * ql, ql), ql)
        gains = jnp.where(d == 0, gain_ref[0:1, wl], gain_ref[1:2, wl])
        entering = sin[d, quarter]
        second = fb[d, 0:1, lanes] * entering.astype(F32) + lk[d, :, lanes]
        for j, state in ((d, entering), (1 - d, second.astype(BF16))):
            n = d * 2 + j
            rows = pl.ds(pl.multiple_of(j * BLOCK, BLOCK), BLOCK)
            carried = jnp.dot(cr_s[n, :, 0:STATE], state, preferred_element_type=F32)
            lead = pltpu.roll(lead_s[n], 128 - 2 * tq * quarter, 1)
            leads = jnp.concatenate(
                [
                    jnp.where(low, lead[:, 2 * t : 2 * t + 1], lead[:, 2 * t + 1 : 2 * t + 2])
                    for t in range(tq)
                ],
                axis=1,
            )
            yv = ys[d, rows, lanes] + leads * carried
            mean = jnp.dot((yv * yv).astype(BF16), ones, preferred_element_type=F32)
            res = yv * lax.rsqrt(mean + 1e-05) * gains
            if last:
                outb[quarter, j] = (res + ys[1 - d, rows, lanes]).astype(BF16)
            else:
                ys[d, rows, lanes] = res

    finish(q, d_a, False)
    for k in range(1, zl):
        in4a[k - 1].wait_recv()
        finish(lax.rem(q + zl - k, zl), d_a, False)
    outs = []
    for k in range(zl):
        quarter = lax.rem(q + zl - k, zl)
        if k > 0:
            in4b[k - 1].wait_recv()
        finish(quarter, d_b, True)
        cols = pl.ds(pl.multiple_of(core * HALF + quarter * ql, ql), ql)
        oc = remote(
            outb.at[quarter, 1 - core], out_ref.at[0, :, cols], o_ss.at[k], o_rs.at[k], partner
        )
        oc.start()
        own = pltpu.make_async_copy(
            outb.at[quarter, core], out_ref.at[0, :, cols], own_sem.at[k]
        )
        own.start()
        outs.append((oc, own))
    for oc, own in outs:
        own.wait()
        oc.wait()
    for c in sent:
        c.wait_send()


def solution(mesh):
    nx, ny, seqs = mesh.shape["fsdp"], mesh.shape["batch"], mesh.shape["seq"]
    nz = seqs // 4
    zl = 4 if nz % 4 == 0 and nz > 4 else 2
    zh_n = nz // zl
    ql = HALF // zl
    cfg = (nx, ny, nz, zl, zh_n, seqs)

    def on_device(hidden, in_weight, marks, cw, cb, dtb, dec, skip, gain):
        kb = in_weight.shape[0]
        hbm = pl.BlockSpec(memory_space=pl.ANY)
        dma = pltpu.SemaphoreType.DMA
        return pl.pallas_call(
            functools.partial(kernel, cfg),
            out_shape=jax.ShapeDtypeStruct(hidden.shape, BF16),
            in_specs=[hbm] * 9,
            out_specs=hbm,
            scratch_shapes=[
                pltpu.SMEM(marks.shape, jnp.int32),
                pltpu.VMEM(cw.shape, F32),
                pltpu.VMEM(cb.shape, F32),
                pltpu.VMEM(dtb.shape, F32),
                pltpu.VMEM(dec.shape, F32),
                pltpu.SMEM(skip.shape, F32),
                pltpu.VMEM(gain.shape, F32),
                pltpu.VMEM((nx, ny, 3 * PART, kb), BF16),
                pltpu.VMEM((ROWS, INNER), BF16),
                pltpu.VMEM((ROWS, HALF + 256), F32),
                pltpu.VMEM((ROWS, 128), BF16),
                pltpu.VMEM((ROWS, 128), BF16),
                pltpu.VMEM((2, 2 * BLOCK, HALF), BF16),
                pltpu.VMEM((2, 2 * BLOCK, HALF), F32),
                pltpu.VMEM((2, STATE, HALF), F32),
                pltpu.VMEM((2, zl, STATE, ql), BF16),
                pltpu.VMEM((2, zl, 1, ql), F32),
                pltpu.VMEM((2, 8, HALF), F32),
                pltpu.VMEM((2, zl, STATE, ql), BF16),
                pltpu.VMEM((2, zl, 1, ql), F32),
                pltpu.VMEM((2, zh_n, STATE, ql), BF16),
                pltpu.VMEM((2, zh_n, 1, ql), F32),
                pltpu.VMEM((STATE, ql), BF16),
                pltpu.VMEM((STATE, ql), BF16),
                pltpu.VMEM((2, zl, STATE, ql), BF16),
                pltpu.VMEM((2, zl, STATE, ql), BF16),
                pltpu.VMEM((zl, 2, BLOCK, ql), BF16),
                pltpu.VMEM((8, 128), F32),
                pltpu.VMEM((4, 128, 128), F32),
                pltpu.VMEM((4, 128, 128), F32),
                pltpu.VMEM((4, 128, 128), F32),
                pltpu.VMEM((4, 128, 128), F32),
                pltpu.VMEM((4, 128, 128), F32),
                pltpu.VMEM((4, 128, 128), F32),
                pltpu.VMEM((4, STATE, 128), BF16),
                pltpu.VMEM((4, 128, 128), BF16),
                pltpu.VMEM((4, 8, 128), F32),
                dma((64,)),
                dma((64,)),
                dma((4,)),
                dma((4,)),
                dma((2, 4, 4)),
                dma((2, 4, 4)),
                dma((2, 3, 2)),
                dma((2, 3, 2)),
                dma((13,)),
                dma((4,)),
                dma((4,)),
                dma((4,)),
            ],
            compiler_params=pltpu.CompilerParams(
                collective_id=0, has_side_effects=True, vmem_limit_bytes=67043328
            ),
        )(hidden, in_weight.T, marks, cw, cb, dtb, dec, skip, gain)

    group = P(("fsdp", "batch"), "seq", None)
    rows = P(("fsdp", "batch"), None)
    return jax.shard_map(
        on_device,
        mesh=mesh,
        in_specs=(group, rows, rows, P(), P(), P(), P(), P(), P()),
        out_specs=group,
        check_vma=False,
    )
```
